32 devices in a mesh: space: 4 (over z), energy: 8 (over y, x, core).
Axes of the slice: x: 2, y: 2, z: 4, core: 2. Of those that a mesh axis runs over, the one named last changes fastest.
Arguments:
- retain: float32 [8, 8], P('space', 'energy'), may hold values from 0.12 to 0.89
- hopping: float32 [8, 8, 2, 128, 128], P('space', 'energy'), may hold values from -0.125 to 0.125
- source: float32 [8, 8, 2, 128, 128], P('space', 'energy'), may hold values from -0.9 to 0.9
- screened: float32 [8, 8, 2, 16384], P('space', None, None, 'energy'), may hold values from -2 to 2
Outputs:
- greens: float32 [8, 8, 2, 128, 128], P('space', 'energy')
- self_energy: float32 [8, 8, 2, 16384], P('space', None, None, 'energy')
The draws below stay inside these ranges and needn't reach their ends.
All inputs are finite; a program needn't handle non-finite values.
Results may differ from the reference program's by a relative error of at most 0.0001.
Values sent between devices are 32-bit elements; how exact they have to be, the bound alone decides.
A program may use at most 64 MiB of HBM per device.

```python
import math
import jax
import jax.numpy as jnp
from jax import lax

M = 128
SLAB_COUNT = 8
ENERGY_COUNT = 8


def draw_retain(key, part):
    root_random_key = jax.random.fold_in(key, 11)
    wobble_random_key, quick_random_key, spike_random_key, damping_random_key = jax.random.split(root_random_key, 4)
    jitter = jnp.exp(jax.random.uniform(wobble_random_key, (SLAB_COUNT, ENERGY_COUNT), jnp.float32, math.log(0.5), math.log(2.0)))
    fast_share = 0.5
    fast_mask = jax.random.uniform(quick_random_key, (1, ENERGY_COUNT), jnp.float32) < fast_share
    slow_rate = jnp.exp(-0.5 * jitter / SLAB_COUNT)
    fast_rate = jnp.exp(-0.8 * jitter)
    noise_amplitude = jnp.where(fast_mask, fast_rate, slow_rate)
    spike_slab_list = jax.random.randint(spike_random_key, (2,), 0, SLAB_COUNT)
    slab_ordinals = jnp.arange(SLAB_COUNT)[:, None]
    spike_slab_mask = (slab_ordinals == spike_slab_list[0]) | (slab_ordinals == spike_slab_list[1])
    spike_loss_factor = jax.random.uniform(damping_random_key, (SLAB_COUNT, ENERGY_COUNT), jnp.float32, 0.5, 0.8)
    noise_amplitude = jnp.where(spike_slab_mask, noise_amplitude * jnp.sqrt(spike_loss_factor), noise_amplitude)
    return (noise_amplitude / 1.125).astype(jnp.float32)


def level_of(stream_key, dims, shards, low, high):
    factor_of = 1.0
    for dim, shards_of in shards:
        heights = jax.random.uniform(jax.random.fold_in(jax.random.fold_in(stream_key, 6), dim), (shards_of,), jnp.float32, low / len(shards), high / len(shards))
        factor_of = factor_of * jnp.repeat(jnp.exp(heights), dims[dim] // shards_of).reshape((-1,) + (1,) * (len(dims) - 1 - dim))
    return factor_of


def noise(rng, extent, deviation, limit, pieces=(), kind=jnp.bfloat16):
    drawn = deviation * jax.random.normal(rng, extent, jnp.float32)
    if pieces:
        drawn = drawn * level_of(rng, extent, pieces, -0.22, 0.18)
    return jnp.clip(drawn, -limit, limit).astype(kind)


def setup_inputs(seed: int = 0) -> dict:
    streams_of = jax.random.split(jax.random.key(seed), 5)
    return {
        "retain": draw_retain(jax.random.fold_in(streams_of[4], 71), 0),
        "hopping": noise(streams_of[1], (SLAB_COUNT, ENERGY_COUNT, 2, M, M), (16 * M) ** -0.5, 0.125, ((0, 4), (1, 8)), jnp.float32),
        "source": noise(streams_of[2], (SLAB_COUNT, ENERGY_COUNT, 2, M, M), 0.15, 0.9, ((0, 4), (1, 8)), jnp.float32),
        "screened": noise(streams_of[3], (SLAB_COUNT, ENERGY_COUNT, 2, M * M), ENERGY_COUNT ** -0.5, 2.0, ((0, 4), (3, 8)), jnp.float32),
    }


EXACT_PRECISION = lax.Precision.HIGHEST


def build_coupler(retain_slab, hop_slab):
    size = hop_slab.shape[-1]
    diagonal_ones = jnp.eye(size, dtype=jnp.float32)
    factor = retain_slab[:, None, None]
    return jnp.stack([factor * (diagonal_ones + hop_slab[:, 0]), factor * hop_slab[:, 1]], axis=1)


def complex_product(left_matrix, right_matrix):
    real_component = jnp.einsum("eij,ejk->eik", left_matrix[:, 0], right_matrix[:, 0], precision=EXACT_PRECISION) - jnp.einsum("eij,ejk->eik", left_matrix[:, 1], right_matrix[:, 1], precision=EXACT_PRECISION)
    imaginary_component = jnp.einsum("eij,ejk->eik", left_matrix[:, 0], right_matrix[:, 1], precision=EXACT_PRECISION) + jnp.einsum("eij,ejk->eik", left_matrix[:, 1], right_matrix[:, 0], precision=EXACT_PRECISION)
    return jnp.stack([real_component, imaginary_component], axis=1)


def times_dagger(left_matrix, right_matrix):
    real_component = jnp.einsum("eij,ekj->eik", left_matrix[:, 0], right_matrix[:, 0], precision=EXACT_PRECISION) + jnp.einsum("eij,ekj->eik", left_matrix[:, 1], right_matrix[:, 1], precision=EXACT_PRECISION)
    imaginary_component = jnp.einsum("eij,ekj->eik", left_matrix[:, 1], right_matrix[:, 0], precision=EXACT_PRECISION) - jnp.einsum("eij,ekj->eik", left_matrix[:, 0], right_matrix[:, 1], precision=EXACT_PRECISION)
    return jnp.stack([real_component, imaginary_component], axis=1)


def sandwich(coupler, middle):
    return times_dagger(complex_product(coupler, middle), coupler)


def reference(retain, hopping, source, screened):
    def slab_step(entering, slab_data):
        retain_slab, hop_slab, fresh_source = slab_data
        coupler = build_coupler(retain_slab, hop_slab)
        leaving = sandwich(coupler, entering) + fresh_source
        return leaving, leaving

    start_block = jnp.zeros((ENERGY_COUNT, 2, M, M), jnp.float32)
    _, greens = lax.scan(slab_step, start_block, (retain, hopping, source))
    pair_blocks = greens.reshape(SLAB_COUNT, ENERGY_COUNT, 2, M * M)

    def convolve(slab_data):
        green_slab, screen_slab = slab_data
        padded = jnp.concatenate([jnp.zeros_like(green_slab), green_slab], axis=0)

        def add_term(boson_index, running_sum):
            shifted = lax.dynamic_slice_in_dim(padded, (ENERGY_COUNT - boson_index).astype(jnp.int32), ENERGY_COUNT, 0)
            weight = lax.dynamic_slice_in_dim(screen_slab, boson_index.astype(jnp.int32), 1, 0)
            real_component = shifted[:, 0] * weight[:, 0] - shifted[:, 1] * weight[:, 1]
            imaginary_component = shifted[:, 0] * weight[:, 1] + shifted[:, 1] * weight[:, 0]
            return running_sum + jnp.stack([real_component, imaginary_component], axis=1)

        return lax.fori_loop(0, ENERGY_COUNT, add_term, jnp.zeros_like(green_slab))

    self_energy = lax.map(convolve, (pair_blocks, screened))
    return greens, self_energy
```

```python
import functools

import jax
import jax.numpy as jnp
from jax import lax
from jax.experimental import pallas as pl
from jax.experimental.pallas import tpu as pltpu
from jax.sharding import PartitionSpec as P

MESH = pl.DeviceIdType.MESH
F32 = jnp.float32
BF16 = jnp.bfloat16
CHUNKS = 8
GROUPS = 4
OUTS = 2
LEAD = 1
ORDER = {6: 0, 4: 1, 7: 2, 5: 3, 2: 4, 3: 5, 1: 1 << 30}
NN = (((1,), (0,)), ((), ()))


def split(value):
    high = value.astype(BF16)
    return high, (value - high.astype(F32)).astype(BF16)


def product(left, right, dims=NN):
    dot = functools.partial(lax.dot_general, dimension_numbers=dims, preferred_element_type=F32)
    (lh, ll), (rh, rl) = left, right
    return dot(lh, rh) + (dot(lh, rl) + dot(ll, rh))


def left_form(real, imag):
    return jnp.concatenate(
        [jnp.concatenate([real, -imag], 1), jnp.concatenate([imag, real], 1)], 0
    )


def dagger_form(real, imag):
    real, imag = real.T, imag.T
    return jnp.concatenate(
        [jnp.concatenate([real, -imag], 1), jnp.concatenate([imag, real], 1)], 0
    )


def kernel(
    retain_hbm, hop_hbm, src_hbm, scr_hbm, g, out_se,
    retain, slabs_in, scr, lefts, rights, bases, entering, landed, own, early,
    load_sem, chain_send, chain_recv, swap_send, swap_recv, ahead_sem, turn,
):
    _, slabs, _, size, _ = slabs_in.shape
    energies, rows = landed.shape[1], landed.shape[3]
    space, energy = lax.axis_index("space"), lax.axis_index("energy")
    stages = lax.axis_size("space")
    piece = size // CHUNKS
    last = slabs - 1
    even = energies % 2 == 0
    power = energies & (energies - 1) == 0
    partner = energy + 1 - 2 * lax.rem(energy, 2)
    second = lax.rem(energy, 2) == 0
    middle = (space > 0) & (space < stages - 1)
    odd = lax.rem(space, 2) == 1
    leaps = second & odd & (space < stages - 2)
    gives = second & middle & jnp.logical_not(odd)
    takes = second & odd & (space > 1)
    hop, src = slabs_in.at[0], slabs_in.at[1]

    loads = [
        pltpu.make_async_copy(hop_hbm.at[:, 0], hop, load_sem.at[0]),
        pltpu.make_async_copy(src_hbm.at[:, 0], src, load_sem.at[0]),
        pltpu.make_async_copy(scr_hbm, scr, load_sem.at[1]),
        pltpu.make_async_copy(retain_hbm, retain, load_sem.at[2]),
    ]
    for load in loads:
        load.start()

    barrier = pltpu.get_barrier_semaphore()
    for step in range(1, energies):
        pl.semaphore_signal(
            barrier, inc=1, device_id=(space, lax.rem(energy + step, energies)), device_id_type=MESH
        )

    @pl.when(space > 0)
    def _():
        pl.semaphore_signal(barrier, inc=1, device_id=(space - 1, energy), device_id_type=MESH)

    @pl.when(takes)
    def _():
        pl.semaphore_signal(barrier, inc=1, device_id=(space - 2, energy), device_id_type=MESH)

    loads[3].wait()
    pltpu.make_async_copy(slabs_in, slabs_in, load_sem.at[0]).wait()

    eye = (
        lax.broadcasted_iota(jnp.int32, (size, size), 0)
        == lax.broadcasted_iota(jnp.int32, (size, size), 1)
    ).astype(F32)
    couplers = []
    for j in range(slabs):
        factor = retain[j]
        couplers.append((factor * (eye + hop[j, 0]), factor * hop[j, 1]))

    def sandwich(left, right, real, imag):
        turned = product(split(jnp.concatenate([real, imag], 1)), right)
        return product(left, split(jnp.concatenate([turned[:, :size], turned[:, size:]], 0)))

    base = jnp.concatenate([src[0, 0], src[0, 1]], 0)
    bases[0] = base
    step_lefts = [None]
    for j in range(1, slabs):
        step_left = split(left_form(*couplers[j]))
        step_right = split(dagger_form(*couplers[j]))
        step_lefts.append(step_left)
        base = sandwich(step_left, step_right, base[:size], base[size:]) + jnp.concatenate(
            [src[j, 0], src[j, 1]], 0
        )
        bases[j] = base

    def chain(lines, reach, sem):
        return pltpu.make_async_remote_copy(
            src_ref=g.at[last, :, lines],
            dst_ref=entering.at[:, lines],
            send_sem=chain_send.at[sem],
            recv_sem=chain_recv.at[lines.start // (size // GROUPS)],
            device_id=(space + reach, energy),
            device_id_type=MESH,
        )

    def send_on(first, count, reach=1):
        for c in range(first, first + count):
            chain(pl.ds(c * piece, piece), reach, int(c == LEAD)).start()

    def sent(times):
        for _ in range(times):
            chain(pl.ds(0, piece), 1, 1).wait_send()
            chain(pl.ds(0, size - piece), 1, 0).wait_send()

    def ahead(i):
        return pltpu.make_async_remote_copy(
            src_ref=own.at[i],
            dst_ref=early.at[i],
            send_sem=ahead_sem.at[0],
            recv_sem=ahead_sem.at[1],
            device_id=(space + 1, energy),
            device_id_type=MESH,
        )

    def aheads():
        return pltpu.make_async_remote_copy(
            src_ref=own,
            dst_ref=early,
            send_sem=ahead_sem.at[0],
            recv_sem=ahead_sem.at[1],
            device_id=(space + 1, energy),
            device_id_type=MESH,
        )

    def swap(j, peer):
        return pltpu.make_async_remote_copy(
            src_ref=g.at[j, :, pl.ds(pl.multiple_of(peer * rows, rows), rows)],
            dst_ref=landed.at[j, energy],
            send_sem=swap_send.at[0],
            recv_sem=swap_recv.at[j],
            device_id=(space, peer),
            device_id_type=MESH,
        )

    def keep(j, real, imag):
        for ref, form in ((lefts, left_form), (rights, dagger_form)):
            high, low = split(form(real, imag))
            ref[j, 0] = high
            ref[j, 1] = low

    def put(j, block):
        g[j, 0] = block[:size]
        g[j, 1] = block[size:]

    def spread(j):
        order = sorted(range(1, energies), key=lambda k: ORDER.get(k, k))
        for k in order:
            swap(j, jnp.bitwise_xor(energy, k) if power else lax.rem(energy + k, energies)).start()

    @pl.when(space > 0)
    def _():
        real, imag = couplers[0]
        for j in range(slabs):
            if j > 0:
                both = product(step_lefts[j], split(jnp.concatenate([real, imag], 0)))
                real, imag = both[:size], both[size:]
            keep(j, real, imag)

        @pl.when(gives)
        def _():
            own[0] = jnp.concatenate([real, imag], 0)
            own[1] = bases[last]

    pl.semaphore_wait(
        barrier,
        energies - 1 + (space < stages - 1).astype(jnp.int32) + leaps.astype(jnp.int32),
    )

    def give_turn():
        pl.semaphore_signal(turn, inc=1, device_id=(space, partner), device_id_type=MESH)

    @pl.when(space == 0)
    def _():
        put(last, bases[last])
        if stages > 1 and even:
            @pl.when(second)
            def _():
                pl.semaphore_wait(turn, 1)
                send_on(0, CHUNKS)
                give_turn()

            @pl.when(jnp.logical_not(second))
            def _():
                send_on(0, CHUNKS)
                chain(pl.ds(0, piece), 1, 1).wait_send()
                give_turn()
        elif stages > 1:
            send_on(0, CHUNKS)

        for j in range(last - 1, -1, -1):
            put(j, bases[j])
        if stages > 1 and even:
            @pl.when(jnp.logical_not(second))
            def _():
                pl.semaphore_wait(turn, 1)
        for j in range(last, -1, -1):
            spread(j)

    @pl.when(space > 0)
    def _():
        @pl.when(gives)
        def _():
            ahead(0).start()
            ahead(1).start()

        @pl.when(takes)
        def _():
            aheads().wait_recv()
            before = split(early[0])
            for j in range(slabs):
                left = lefts[j, 0], lefts[j, 1]
                right = rights[j, 0], rights[j, 1]
                bases[j] = sandwich(left, right, early[1, :size], early[1, size:]) + bases[j]
                both = product(left, before)
                keep(j, both[:size], both[size:])

        turned = []
        for c in range(GROUPS):
            lines = pl.ds(c * (size // GROUPS), size // GROUPS)
            chain(lines, 1, 0).wait_recv()
            arrived = split(jnp.concatenate([entering[0, lines], entering[1, lines]], 1))
            turned.append(product(arrived, (rights[last, 0], rights[last, 1])))
        turned = jnp.concatenate(turned, 0)
        inner = split(jnp.concatenate([turned[:, :size], turned[:, size:]], 0))
        height = size // OUTS
        for o in range(OUTS):
            for part in range(2):
                lines = slice(part * size + o * height, part * size + (o + 1) * height)
                left = lefts[last, 0, lines], lefts[last, 1, lines]
                g[last, part, o * height : (o + 1) * height] = (
                    product(left, inner) + bases[last, lines]
                )

            @pl.when(middle & jnp.logical_not(second))
            def _():
                send_on(o * CHUNKS // OUTS, CHUNKS // OUTS)

            @pl.when(leaps)
            def _():
                send_on(o * CHUNKS // OUTS, CHUNKS // OUTS, 2)

        @pl.when(second & odd & middle)
        def _():
            send_on(0, CHUNKS)
            if even:
                give_turn()

        def rest():
            for j in range(last - 1, -1, -1):
                put(
                    j,
                    sandwich(
                        (lefts[j, 0], lefts[j, 1]),
                        (rights[j, 0], rights[j, 1]),
                        entering[0],
                        entering[1],
                    )
                    + bases[j],
                )

        if even:
            @pl.when(jnp.logical_not(second) & odd & middle)
            def _():
                pl.semaphore_wait(turn, 1)
        spread(last)
        rest()
        for j in range(last - 1, -1, -1):
            spread(j)

    def lanes(part):
        return pl.ds(part, rows, stride=2)

    loads[2].wait()
    mine = pl.ds(pl.multiple_of(energy * rows, rows), rows)
    for j in range(last, -1, -1):
        landed[j, energy] = g[j, :, mine]
        others = landed.at[j, pl.ds(0, energies - 1)]
        pltpu.make_async_copy(others, others, swap_recv.at[j]).wait()
        for e in range(energies):
            real = jnp.zeros((rows, size), F32)
            imag = jnp.zeros((rows, size), F32)
            for w in range(e + 1):
                gr, gi = landed[j, e - w, 0], landed[j, e - w, 1]
                sr, si = scr[j, w, lanes(0)], scr[j, w, lanes(1)]
                real = real + (gr * sr - gi * si)
                imag = imag + (gr * si + gi * sr)
            out_se[j, e, lanes(0)] = real
            out_se[j, e, lanes(1)] = imag

    others = landed.at[:, pl.ds(0, energies - 1)]
    pltpu.make_async_copy(others, others, swap_send.at[0]).wait()

    @pl.when(gives)
    def _():
        aheads().wait_send()

    if even:
        @pl.when((space == 0) & jnp.logical_not(second) & (stages > 1))
        def _():
            chain(pl.ds(0, size - piece), 1, 0).wait_send()

        @pl.when(((space == 0) & second & (stages > 1)) | (middle & (jnp.logical_not(second) | odd)))
        def _():
            sent(1)
    else:
        @pl.when((space == 0) & (stages > 1) | (middle & (jnp.logical_not(second) | odd)))
        def _():
            sent(1)

    @pl.when(leaps)
    def _():
        sent(1)


def write_out(g, se, out_g, out_se, sems):
    copies = [
        pltpu.make_async_copy(g, out_g.at[:, 0], sems.at[0]),
        pltpu.make_async_copy(se, out_se, sems.at[1]),
    ]
    for copy in copies:
        copy.start()
    for copy in copies:
        copy.wait()


def body(retain, hopping, source, screened):
    slabs, _, _, size, _ = hopping.shape
    energies = screened.shape[1]
    rows = screened.shape[3] // size
    woven = (
        screened.reshape(slabs, energies, 2, rows, size)
        .transpose(0, 1, 3, 2, 4)
        .reshape(slabs, energies, 2 * rows, size)
    )
    any_spec = pl.BlockSpec(memory_space=pl.ANY)
    vmem_spec = pl.BlockSpec(memory_space=pltpu.VMEM)
    vmem = pltpu.VMEM
    greens, self_energy = pl.pallas_call(
        kernel,
        out_shape=(vmem((slabs, 2, size, size), F32), vmem(woven.shape, F32)),
        in_specs=[pl.BlockSpec(memory_space=pltpu.HBM)] * 4,
        out_specs=(vmem_spec, vmem_spec),
        scratch_shapes=[
            pltpu.SMEM((slabs,), F32),
            vmem((2, slabs, 2, size, size), F32),
            vmem(woven.shape, F32),
            vmem((slabs, 2, 2 * size, 2 * size), BF16),
            vmem((slabs, 2, 2 * size, 2 * size), BF16),
            vmem((slabs, 2 * size, size), F32),
            vmem((2, size, size), F32),
            vmem((slabs, energies, 2, rows, size), F32),
            vmem((2, 2 * size, size), F32),
            vmem((2, 2 * size, size), F32),
            pltpu.SemaphoreType.DMA((3,)),
            pltpu.SemaphoreType.DMA((2,)),
            pltpu.SemaphoreType.DMA((GROUPS,)),
            pltpu.SemaphoreType.DMA((1,)),
            pltpu.SemaphoreType.DMA((slabs,)),
            pltpu.SemaphoreType.DMA((2,)),
            pltpu.SemaphoreType.REGULAR,
        ],
        compiler_params=pltpu.CompilerParams(
            collective_id=0, has_side_effects=True
        ),
    )(retain.reshape(slabs), hopping, source, woven)
    greens, self_energy = pl.pallas_call(
        write_out,
        out_shape=(
            jax.ShapeDtypeStruct(source.shape, F32),
            jax.ShapeDtypeStruct(woven.shape, F32),
        ),
        in_specs=[vmem_spec, vmem_spec],
        out_specs=(any_spec, any_spec),
        scratch_shapes=[pltpu.SemaphoreType.DMA((2,))],
        compiler_params=pltpu.CompilerParams(vmem_limit_bytes=4 << 20),
    )(greens, self_energy)
    return greens, (
        self_energy.reshape(slabs, energies, rows, 2, size)
        .transpose(0, 1, 3, 2, 4)
        .reshape(screened.shape)
    )


def solution(mesh):
    placed = (
        P("space", "energy"),
        P("space", "energy", None, None, None),
        P("space", "energy", None, None, None),
        P("space", None, None, "energy"),
    )
    return jax.shard_map(
        body,
        mesh=mesh,
        in_specs=placed,
        out_specs=(P("space", "energy", None, None, None), P("space", None, None, "energy")),
        check_vma=False,
    )
```

```python
import functools

import jax
import jax.numpy as jnp
from jax import lax
from jax.experimental import pallas as pl
from jax.experimental.pallas import tpu as pltpu
from jax.sharding import PartitionSpec as P

MESH = pl.DeviceIdType.MESH
F32 = jnp.float32
BF16 = jnp.bfloat16
CHUNKS = 8
GROUPS = 4
OUTS = 2
ORDER = {6: 0, 4: 1, 7: 2, 5: 3, 2: 4, 3: 5, 1: 1 << 30}


def split(value):
    high = value.astype(BF16)
    return high, (value - high.astype(F32)).astype(BF16)


dot = functools.partial(
    lax.dot_general, dimension_numbers=(((1,), (0,)), ((), ())), preferred_element_type=F32
)


def rows_by(block, right):
    (high, low), (rh, rl) = split(block), right
    count = high.shape[0]
    both = dot(jnp.concatenate([high, low], 0), rh)
    return both[:count] + (dot(high, rl) + both[count:])


def left_form(real, imag):
    return jnp.concatenate(
        [jnp.concatenate([real, -imag], 1), jnp.concatenate([imag, real], 1)], 0
    )


def dagger_form(real, imag):
    real, imag = real.T, imag.T
    return jnp.concatenate(
        [jnp.concatenate([real, -imag], 1), jnp.concatenate([imag, real], 1)], 0
    )


def arranged(form):
    size = form.shape[0] // 2
    height = size // OUTS
    high, low = split(form)
    return [
        jnp.concatenate(
            [x[p * size + o * height : p * size + (o + 1) * height] for x in (high, low) for p in range(2)], 0
        )
        for o in range(OUTS)
    ]


def part_by(left, right):
    height, size = left.shape[0] // 4, right.shape[1] // 2
    product = dot(left, right)
    cross = product[: 2 * height, size:] + product[2 * height :, :size]
    both = product[: 2 * height, :size] + cross
    return both[:height], both[height:]


def columns_by(left, block):
    right = stacked(block)
    parts = [part_by(x, right) for x in left]
    return jnp.concatenate([p[0] for p in parts] + [p[1] for p in parts], 0)


def stacked(block):
    return jnp.concatenate(split(block), 1)


def turned_block(turned):
    size = turned.shape[1] // 2
    return jnp.concatenate([turned[:, :size], turned[:, size:]], 0)


def kernel(
    retain_hbm, hop_hbm, src_hbm, scr_hbm, g, out_se,
    retain, slabs_in, scr, lefts, rights, bases, entering, landed, own, early, guest, passed, spun,
    load_sem, chain_send, chain_recv, guest_recv, swap_send, swap_recv, ahead_sem, turn,
):
    _, slabs, _, size, _ = slabs_in.shape
    energies, rows = landed.shape[1], landed.shape[3]
    space, energy = lax.axis_index("space"), lax.axis_index("energy")
    stages = lax.axis_size("space")
    piece, height, group = size // CHUNKS, size // OUTS, size // GROUPS
    last = slabs - 1
    paired = energies % 2 == 0
    power = energies & (energies - 1) == 0 and energies >= OUTS
    order = sorted(range(1, energies), key=lambda k: ORDER.get(k, k))
    hop, src = slabs_in.at[0], slabs_in.at[1]

    odd = lax.rem(space, 2) == 1
    middle = (space > 0) & (space < stages - 1)
    if paired:
        partner = energy + 1 - 2 * lax.rem(energy, 2)
        second = lax.rem(energy, 2) == 0
    else:
        partner = energy
        second = energy < 0
    first = jnp.logical_not(second)
    hosts = first & odd & middle & paired
    hosted = second & odd & middle
    gives = second & middle & jnp.logical_not(odd)
    takes = second & odd & (space > 1)
    leaps = hosts & (space + 2 < stages)
    carries = (first & (space < stages - 1)) | (second & (space == 0) & (stages > 1))
    stops = (space == stages - 1) | gives

    loads = [
        pltpu.make_async_copy(retain_hbm, retain, load_sem.at[2]),
        pltpu.make_async_copy(hop_hbm.at[:, 0], hop, load_sem.at[0]),
        pltpu.make_async_copy(src_hbm.at[:, 0], src, load_sem.at[0]),
        pltpu.make_async_copy(scr_hbm, scr, load_sem.at[1]),
    ]
    for load in loads:
        load.start()

    barrier = pltpu.get_barrier_semaphore()

    def greet(where, who):
        pl.semaphore_signal(barrier, inc=1, device_id=(where, who), device_id_type=MESH)

    for step in range(1, energies):
        greet(space, lax.rem(energy + step, energies))

    @pl.when((first & (space > 0)) | takes)
    def _():
        greet(space - 1, energy)

    if paired:
        @pl.when(((space == 1) & hosts) | (second & (space > 0) & jnp.logical_not(odd)))
        def _():
            greet(space - 1, partner)

        @pl.when((space == 1) & second & (stages == 2))
        def _():
            greet(space - 1, energy)

        @pl.when(hosts & (space > 1))
        def _():
            greet(space - 2, energy)

        @pl.when(takes & (space == stages - 1))
        def _():
            greet(space - 2, partner)

    greeted = (
        energies - 1
        + carries.astype(jnp.int32)
        + hosts.astype(jnp.int32)
        + leaps.astype(jnp.int32)
        + gives.astype(jnp.int32)
    )

    def enter():
        pl.semaphore_wait(barrier, greeted)

    loads[0].wait()
    pltpu.make_async_copy(slabs_in, slabs_in, load_sem.at[0]).wait()

    eye = (
        lax.broadcasted_iota(jnp.int32, (size, size), 0)
        == lax.broadcasted_iota(jnp.int32, (size, size), 1)
    ).astype(F32)
    couplers = []
    for j in range(slabs):
        factor = retain[j]
        couplers.append((factor * (eye + hop[j, 0]), factor * hop[j, 1]))

    def sandwich(left, right, block):
        wide = jnp.concatenate([block[:size], block[size:]], 1)
        return columns_by(left, turned_block(rows_by(wide, right)))

    def source(j):
        return jnp.concatenate([src[j, 0], src[j, 1]], 0)

    step_lefts, step_rights = [None], [None]
    for j in range(1, slabs):
        step_lefts.append(arranged(left_form(*couplers[j])))
        step_rights.append(split(dagger_form(*couplers[j])))

    def copy(source_ref, target_ref, sems, where, who, wait=0):
        return pltpu.make_async_remote_copy(
            src_ref=source_ref,
            dst_ref=target_ref,
            send_sem=sems[0],
            recv_sem=sems[1],
            device_id=(where, who),
            device_id_type=MESH,
        )

    def line(source_ref, target_ref, recv, start, count, where, who, sem=0):
        lines = pl.ds(start, count)
        return copy(
            source_ref.at[:, lines],
            target_ref.at[:, lines],
            (chain_send.at[sem], recv.at[start // group]),
            where,
            who,
        )

    made = g.at[last]

    def send_on(begin, count, to_guest=False):
        for c in range(begin, begin + count):
            if to_guest:
                line(made, guest, guest_recv, c * piece, piece, space + 1, partner).start()
            else:
                line(made, entering, chain_recv, c * piece, piece, space + 1, energy, sem=int(c == 0)).start()

    def sent(count, sem=0):
        line(made, entering, chain_recv, 0, count, space, energy, sem=sem).wait_send()

    def ahead(refs, where, who):
        return copy(refs[0], refs[1], (ahead_sem.at[0], ahead_sem.at[1]), where, who)

    def hand(where, who):
        for i in range(2):
            ahead((own.at[i], early.at[i]), where, who).start()

    def swap(j, peer):
        return copy(
            g.at[j, :, pl.ds(pl.multiple_of(peer * rows, rows), rows)],
            landed.at[j, energy],
            (swap_send.at[0], swap_recv.at[j]),
            space,
            peer,
        )

    def spread(j):
        for k in order:
            swap(j, jnp.bitwise_xor(energy, k) if power else lax.rem(energy + k, energies)).start()

    def part_spread(j, o):
        half = energies // OUTS
        near = [k for k in order if k < half]
        far = [k for k in order if half <= k]
        for ks, there in ((near, energy // half == o), (far, energy // half != o)):
            @pl.when(there)
            def _():
                for k in ks:
                    swap(j, jnp.bitwise_xor(energy, k)).start()

    def keep(j, block):
        real, imag = block[:size], block[size:]
        for o, part in enumerate(arranged(left_form(real, imag))):
            lefts[j, o] = part
        rights[j, 0], rights[j, 1] = split(dagger_form(real, imag))

    def left_of(j):
        return [lefts[j, o] for o in range(OUTS)]

    def right_of(j):
        return rights[j, 0], rights[j, 1]

    def finish(target, o, left, inner, more):
        for part, value in enumerate(part_by(left, inner)):
            target[part, o * height : (o + 1) * height] = value + more(part)

    def base_part(j, o):
        return lambda part: bases[j, part * size + o * height : part * size + (o + 1) * height]

    def give_turn():
        pl.semaphore_signal(turn, inc=1, device_id=(space, partner), device_id_type=MESH)

    @pl.when(space == 0)
    def _():
        base = source(0)
        for j in range(1, slabs):
            g[j - 1, 0] = base[:size]
            g[j - 1, 1] = base[size:]
            if j < last:
                base = sandwich(step_lefts[j], step_rights[j], base) + source(j)
        wide = jnp.concatenate([base[:size], base[size:]], 1)
        inner = stacked(turned_block(rows_by(wide, step_rights[last])))
        for o in range(OUTS):
            finish(
                made,
                o,
                step_lefts[last][o],
                inner,
                lambda part: src[last, part, o * height : (o + 1) * height],
            )
            if o == 0:
                enter()
            if stages > 1:
                @pl.when(first)
                def _():
                    send_on(o * CHUNKS // OUTS, CHUNKS // OUTS)
        if stages > 1 and paired:
            @pl.when(second)
            def _():
                pl.semaphore_wait(turn, 1)
                if stages > 2:
                    send_on(0, CHUNKS, True)
                else:
                    send_on(0, CHUNKS)
                give_turn()

            @pl.when(first)
            def _():
                sent(piece, 1)
                give_turn()
                pl.semaphore_wait(turn, 1)

        for j in range(last, -1, -1):
            spread(j)

    @pl.when(space > 0)
    def _():
        base = source(0)
        bases[0] = base
        for j in range(1, slabs):
            base = sandwich(step_lefts[j], step_rights[j], base) + source(j)
            bases[j] = base
        block = jnp.concatenate(couplers[0], 0)
        for j in range(slabs):
            if j > 0:
                block = columns_by(step_lefts[j], block)
            keep(j, block)

        @pl.when(gives | (hosted & (space == 1)))
        def _():
            own[0] = block
            own[1] = bases[last]
        enter()

        @pl.when(gives)
        def _():
            hand(space + 1, energy)

        @pl.when(takes)
        def _():
            ahead((own, early), space, energy).wait_recv()
            for j in range(slabs):
                left = left_of(j)
                bases[j] = sandwich(left, right_of(j), early[1]) + bases[j]
                block = columns_by(left, early[0])
                keep(j, block)
                if j == last:
                    @pl.when(hosted)
                    def _():
                        own[0] = block
                        own[1] = bases[last]

        if paired:
            @pl.when(hosted)
            def _():
                hand(space, partner)

            @pl.when(hosts)
            def _():
                ahead((own, early), space, energy).wait_recv()
                keep(slabs, early[0])

        turned = []
        for c in range(GROUPS):
            line(made, entering, chain_recv, c * group, group, space, energy).wait_recv()
            lines = pl.ds(c * group, group)
            arrived = jnp.concatenate([entering[0, lines], entering[1, lines]], 1)
            turned.append(rows_by(arrived, right_of(last)))
            if c < GROUPS - 1:
                for j in range(last):
                    spun[j, lines] = rows_by(arrived, right_of(j))

        inner = stacked(turned_block(jnp.concatenate(turned, 0)))
        for o in range(OUTS):
            finish(made, o, lefts[last, o], inner, base_part(last, o))

            @pl.when(middle & first)
            def _():
                send_on(o * CHUNKS // OUTS, CHUNKS // OUTS)

            if power:
                @pl.when(stops)
                def _():
                    part_spread(last, o)

        if paired:
            @pl.when(hosts)
            def _():
                turned = []
                for c in range(GROUPS):
                    line(made, guest, guest_recv, c * group, group, space, energy).wait_recv()
                    line(guest, entering, chain_recv, c * group, group, space, partner).start()
                    lines = pl.ds(c * group, group)
                    arrived = jnp.concatenate([guest[0, lines], guest[1, lines]], 1)
                    turned.append(rows_by(arrived, right_of(slabs)))
                inner = stacked(turned_block(jnp.concatenate(turned, 0)))
                for o in range(OUTS):
                    finish(
                        passed,
                        o,
                        lefts[slabs, o],
                        inner,
                        lambda part: early[
                            1, part * size + o * height : part * size + (o + 1) * height
                        ],
                    )
                    chunks = range(o * CHUNKS // OUTS, (o + 1) * CHUNKS // OUTS)

                    @pl.when(leaps & (space + 2 < stages - 1))
                    def _():
                        for c in chunks:
                            line(passed, guest, guest_recv, c * piece, piece, space + 2, energy).start()

                    @pl.when(leaps & (space + 2 == stages - 1))
                    def _():
                        for c in chunks:
                            line(
                                passed, entering, chain_recv, c * piece, piece, space + 2, partner
                            ).start()

                for c in range(CHUNKS):
                    line(passed, entering, chain_recv, c * piece, piece, space + 1, partner).start()
                give_turn()

            @pl.when(hosted)
            def _():
                pl.semaphore_wait(turn, 1)

        @pl.when(jnp.logical_not(stops) if power else True)
        def _():
            spread(last)

        for j in range(last - 1, -1, -1):
            tail = pl.ds(size - group, group)
            spun[j, tail] = rows_by(arrived, right_of(j))
            inner = stacked(turned_block(spun[j]))
            for o in range(OUTS):
                finish(g.at[j], o, lefts[j, o], inner, base_part(j, o))
                if power:
                    part_spread(j, o)
            if not power:
                spread(j)

    def lanes(part):
        return pl.ds(part, rows, stride=2)

    loads[3].wait()
    mine = pl.ds(pl.multiple_of(energy * rows, rows), rows)
    for j in range(last, -1, -1):
        landed[j, energy] = g[j, :, mine]
        others = landed.at[j, pl.ds(0, energies - 1)]
        pltpu.make_async_copy(others, others, swap_recv.at[j]).wait()
        for e in range(energies):
            real = jnp.zeros((rows, size), F32)
            imag = jnp.zeros((rows, size), F32)
            for w in range(e + 1):
                gr, gi = landed[j, e - w, 0], landed[j, e - w, 1]
                sr, si = scr[j, w, lanes(0)], scr[j, w, lanes(1)]
                real = real + (gr * sr - gi * si)
                imag = imag + (gr * si + gi * sr)
            out_se[j, e, lanes(0)] = real
            out_se[j, e, lanes(1)] = imag

    others = landed.at[:, pl.ds(0, energies - 1)]
    pltpu.make_async_copy(others, others, swap_send.at[0]).wait()

    @pl.when(gives | hosted)
    def _():
        ahead((own, early), space, energy).wait_send()

    @pl.when(first & (space < stages - 1))
    def _():
        sent(size - piece)
        if not paired:
            sent(piece, 1)

    if paired:
        @pl.when(first & middle)
        def _():
            sent(piece, 1)

        @pl.when(second & (space == 0) & (stages > 1))
        def _():
            if stages > 2:
                sent(size)
            else:
                sent(size - piece)
                sent(piece, 1)

        @pl.when(hosts)
        def _():
            sent(size)
            sent(size)

        @pl.when(leaps)
        def _():
            sent(size)


def write_out(g, se, out_g, out_se, sems):
    copies = [
        pltpu.make_async_copy(g, out_g.at[:, 0], sems.at[0]),
        pltpu.make_async_copy(se, out_se, sems.at[1]),
    ]
    for copy in copies:
        copy.start()
    for copy in copies:
        copy.wait()


def body(retain, hopping, source, screened):
    slabs, _, _, size, _ = hopping.shape
    energies = screened.shape[1]
    rows = screened.shape[3] // size
    woven = (
        screened.reshape(slabs, energies, 2, rows, size)
        .transpose(0, 1, 3, 2, 4)
        .reshape(slabs, energies, 2 * rows, size)
    )
    any_spec = pl.BlockSpec(memory_space=pl.ANY)
    vmem_spec = pl.BlockSpec(memory_space=pltpu.VMEM)
    vmem = pltpu.VMEM
    greens, self_energy = pl.pallas_call(
        kernel,
        out_shape=(vmem((slabs, 2, size, size), F32), vmem(woven.shape, F32)),
        in_specs=[pl.BlockSpec(memory_space=pltpu.HBM)] * 4,
        out_specs=(vmem_spec, vmem_spec),
        scratch_shapes=[
            pltpu.SMEM((slabs,), F32),
            vmem((2, slabs, 2, size, size), F32),
            vmem(woven.shape, F32),
            vmem((slabs + 1, OUTS, 4 * size // OUTS, 2 * size), BF16),
            vmem((slabs + 1, 2, 2 * size, 2 * size), BF16),
            vmem((slabs, 2 * size, size), F32),
            vmem((2, size, size), F32),
            vmem((slabs, energies, 2, rows, size), F32),
            vmem((2, 2 * size, size), F32),
            vmem((2, 2 * size, size), F32),
            vmem((2, size, size), F32),
            vmem((2, size, size), F32),
            vmem((max(slabs - 1, 1), size, 2 * size), F32),
            pltpu.SemaphoreType.DMA((3,)),
            pltpu.SemaphoreType.DMA((2,)),
            pltpu.SemaphoreType.DMA((GROUPS,)),
            pltpu.SemaphoreType.DMA((GROUPS,)),
            pltpu.SemaphoreType.DMA((1,)),
            pltpu.SemaphoreType.DMA((slabs,)),
            pltpu.SemaphoreType.DMA((2,)),
            pltpu.SemaphoreType.REGULAR,
        ],
        compiler_params=pltpu.CompilerParams(
            collective_id=0, has_side_effects=True
        ),
    )(retain.reshape(slabs), hopping, source, woven)
    greens, self_energy = pl.pallas_call(
        write_out,
        out_shape=(
            jax.ShapeDtypeStruct(source.shape, F32),
            jax.ShapeDtypeStruct(woven.shape, F32),
        ),
        in_specs=[vmem_spec, vmem_spec],
        out_specs=(any_spec, any_spec),
        scratch_shapes=[pltpu.SemaphoreType.DMA((2,))],
        compiler_params=pltpu.CompilerParams(vmem_limit_bytes=4 << 20),
    )(greens, self_energy)
    return greens, (
        self_energy.reshape(slabs, energies, rows, 2, size)
        .transpose(0, 1, 3, 2, 4)
        .reshape(screened.shape)
    )


def solution(mesh):
    placed = (
        P("space", "energy"),
        P("space", "energy", None, None, None),
        P("space", "energy", None, None, None),
        P("space", None, None, "energy"),
    )
    return jax.shard_map(
        body,
        mesh=mesh,
        in_specs=placed,
        out_specs=(P("space", "energy", None, None, None), P("space", None, None, "energy")),
        check_vma=False,
    )
```

```python
import functools

import jax
import jax.numpy as jnp
from jax import lax
from jax.experimental import pallas as pl
from jax.experimental.pallas import tpu as pltpu
from jax.sharding import PartitionSpec as P

MESH = pl.DeviceIdType.MESH
F32 = jnp.float32
BF16 = jnp.bfloat16
CHUNKS = 8
GROUPS = 4
OUTS = 4
ORDER = {6: 0, 7: 1, 4: 2, 5: 3, 2: 4, 3: 5, 1: 1 << 30}
LS = 4


def split(value):
    high = value.astype(BF16)
    return high, (value - high.astype(F32)).astype(BF16)


dot = functools.partial(
    lax.dot_general, dimension_numbers=(((1,), (0,)), ((), ())), preferred_element_type=F32
)


def rows_by(block, right):
    (high, low), (rh, rl) = split(block), right
    count = high.shape[0]
    both = dot(jnp.concatenate([high, low], 0), rh)
    return both[:count] + (dot(high, rl) + both[count:])


def left_form(real, imag):
    return jnp.concatenate(
        [jnp.concatenate([real, -imag], 1), jnp.concatenate([imag, real], 1)], 0
    )


def dagger_form(real, imag):
    real, imag = real.T, imag.T
    return jnp.concatenate(
        [jnp.concatenate([real, -imag], 1), jnp.concatenate([imag, real], 1)], 0
    )


def arranged(form):
    size = form.shape[0] // 2
    height = size // OUTS
    high, low = split(form)
    return [
        jnp.concatenate(
            [x[p * size + o * height : p * size + (o + 1) * height] for x in (high, low) for p in range(2)], 0
        )
        for o in range(OUTS)
    ]


def part_by(left, right):
    height, size = left.shape[0] // 4, right.shape[1] // 2
    product = dot(left[: 2 * height], right)
    other = dot(left[2 * height :], right[:, :size])
    both = product[:, :size] + (product[:, size:] + other)
    return both[:height], both[height:]


def parts_of(product):
    height, size = product.shape[0] // 4, product.shape[1] // 2
    cross = product[: 2 * height, size:] + product[2 * height :, :size]
    both = product[: 2 * height, :size] + cross
    return both[:height], both[height:]


def columns_by(left, block):
    right = stacked(block)
    parts = [part_by(x, right) for x in left]
    return jnp.concatenate([p[0] for p in parts] + [p[1] for p in parts], 0)


def stacked(block):
    return jnp.concatenate(split(block), 1)


def turned_block(turned):
    size = turned.shape[1] // 2
    return jnp.concatenate([turned[:, :size], turned[:, size:]], 0)


def kernel(
    retain_hbm, hop_hbm, src_hbm, scr_hbm, g, out_se,
    retain, slabs_in, scr, lefts, rights, bases, entering, landed, own, early, guest, passed, spun,
    load_sem, chain_send, chain_recv, guest_recv, swap_send, swap_recv, ahead_sem, turn, ready,
):
    _, slabs, _, size, _ = slabs_in.shape
    energies, rows = landed.shape[1], landed.shape[3]
    space, energy = lax.axis_index("space"), lax.axis_index("energy")
    stages = lax.axis_size("space")
    piece, height, group = size // CHUNKS, size // OUTS, size // GROUPS
    last = slabs - 1
    paired = energies % 2 == 0
    power = energies & (energies - 1) == 0 and paired
    order = sorted(range(1, energies), key=lambda k: ORDER.get(k, k))
    hop, src = slabs_in.at[0], slabs_in.at[1]

    odd = lax.rem(space, 2) == 1
    middle = (space > 0) & (space < stages - 1)
    if paired:
        partner = energy + 1 - 2 * lax.rem(energy, 2)
        second = lax.rem(energy, 2) == 0
    else:
        partner = energy
        second = energy < 0
    first = jnp.logical_not(second)
    hosts = first & odd & middle & paired
    hosted = second & odd & middle
    gives = second & middle & jnp.logical_not(odd)
    takes = second & odd & (space > 1)
    leaps = hosts & (space + 2 < stages)
    carries = (first & (space < stages - 1)) | (second & (space == 0) & (stages > 1))
    stops = (space == stages - 1) | gives

    loads = [
        pltpu.make_async_copy(retain_hbm, retain, load_sem.at[2]),
        *(
            pltpu.make_async_copy(
                array.at[which, 0, part, pl.ds(i * size // LS, size // LS)],
                ref.at[which, part, pl.ds(i * size // LS, size // LS)],
                load_sem.at[0],
            )
            for array, ref, which in (
                (hop_hbm, hop, slice(1, None)),
                (src_hbm, src, slice(0, 1)),
            )
            for part in range(2)
            for i in range(LS)
        ),
        pltpu.make_async_copy(src_hbm.at[1:, 0], src.at[1:], load_sem.at[3]),
        pltpu.make_async_copy(hop_hbm.at[:1, 0], hop.at[:1], load_sem.at[3]),
        pltpu.make_async_copy(scr_hbm, scr, load_sem.at[1]),
    ]
    for load in loads:
        load.start()

    barrier = pltpu.get_barrier_semaphore()

    def greet(where, who):
        pl.semaphore_signal(barrier, inc=1, device_id=(where, who), device_id_type=MESH)

    bits = [1 << b for b in range(energies.bit_length() - 1)] if power else []
    rounds = len(bits) - 1
    if power:
        for bit in bits:
            greet(space, jnp.bitwise_xor(energy, bit))
    else:
        for step in range(1, energies):
            greet(space, lax.rem(energy + step, energies))

    def call(level):
        if 0 < level <= rounds:
            for bit in bits:
                pl.semaphore_signal(
                    ready.at[level - 1],
                    inc=1,
                    device_id=(space, jnp.bitwise_xor(energy, bit)),
                    device_id_type=MESH,
                )

    def hear(level):
        if 0 < level <= rounds:
            pl.semaphore_wait(ready.at[level - 1], len(bits))
            call(level + 1)

    def hear_all():
        for level in range(1, rounds + 1):
            hear(level)

    @pl.when((first & (space > 0)) | takes)
    def _():
        greet(space - 1, energy)

    if paired:
        @pl.when(((space == 1) & hosts) | (second & (space > 0) & jnp.logical_not(odd)))
        def _():
            greet(space - 1, partner)

        @pl.when((space == 1) & second & (stages == 2))
        def _():
            greet(space - 1, energy)

        @pl.when(hosts & (space > 1))
        def _():
            greet(space - 2, energy)

        @pl.when(takes & (space == stages - 1))
        def _():
            greet(space - 2, partner)

    greeted = (
        (len(bits) if power else energies - 1)
        + carries.astype(jnp.int32)
        + hosts.astype(jnp.int32)
        + leaps.astype(jnp.int32)
        + gives.astype(jnp.int32)
    )

    def enter():
        pl.semaphore_wait(barrier, greeted)
        call(1)

    loads[0].wait()
    pltpu.make_async_copy(hop, hop, load_sem.at[0]).wait()

    def settle():
        pltpu.make_async_copy(hop, hop, load_sem.at[3]).wait()

    eye = (
        lax.broadcasted_iota(jnp.int32, (size, size), 0)
        == lax.broadcasted_iota(jnp.int32, (size, size), 1)
    ).astype(F32)

    def coupler(j):
        factor = retain[j]
        return factor * (eye + hop[j, 0]), factor * hop[j, 1]

    def sandwich(left, right, block):
        wide = jnp.concatenate([block[:size], block[size:]], 1)
        return columns_by(left, turned_block(rows_by(wide, right)))

    def source(j):
        return jnp.concatenate([src[j, 0], src[j, 1]], 0)

    step_lefts, step_rights = [None], [None]
    for j in range(1, slabs):
        step_lefts.append(arranged(left_form(*coupler(j))))
        step_rights.append(split(dagger_form(*coupler(j))))

    def copy(source_ref, target_ref, sems, where, who):
        return pltpu.make_async_remote_copy(
            src_ref=source_ref,
            dst_ref=target_ref,
            send_sem=sems[0],
            recv_sem=sems[1],
            device_id=(where, who),
            device_id_type=MESH,
        )

    def line(source_ref, target_ref, recv, start, count, where, who, sem=0):
        lines = pl.ds(start, count)
        return copy(
            source_ref.at[:, lines],
            target_ref.at[:, lines],
            (chain_send.at[sem], recv.at[start // group]),
            where,
            who,
        )

    made = g.at[last]

    def send_on(begin, count, to_guest=False):
        for c in range(begin, begin + count):
            if to_guest:
                line(made, guest, guest_recv, c * piece, piece, space + 1, partner).start()
            else:
                line(made, entering, chain_recv, c * piece, piece, space + 1, energy, sem=int(c == 0)).start()

    def sent(count, sem=0):
        line(made, entering, chain_recv, 0, count, space, energy, sem=sem).wait_send()

    def ahead(refs, where, who):
        return copy(refs[0], refs[1], (ahead_sem.at[0], ahead_sem.at[1]), where, who)

    def hand(where, who):
        for i in range(2):
            ahead((own.at[i], early.at[i]), where, who).start()

    def swap(j, peer):
        return copy(
            g.at[j, :, pl.ds(pl.multiple_of(peer * rows, rows), rows)],
            landed.at[j, energy],
            (swap_send.at[0], swap_recv.at[j]),
            space,
            peer,
        )

    def spread(*js):
        for k in order:
            if not power:
                peer = lax.rem(energy + k, energies)
            elif k == 1:
                peer = jnp.bitwise_xor(energy, 1)
            else:
                peer = jnp.bitwise_xor(energy - lax.rem(energy, 2), k)
            for j in js:
                swap(j, peer).start()

    def keep(j, block):
        real, imag = block[:size], block[size:]
        for o, part in enumerate(arranged(left_form(real, imag))):
            lefts[j, o] = part
        rights[j, 0], rights[j, 1] = split(dagger_form(real, imag))

    def left_of(j):
        return [lefts[j, o] for o in range(OUTS)]

    def right_of(j):
        return rights[j, 0], rights[j, 1]

    def finish(target, o, left, inner, more):
        for part, value in enumerate(part_by(left, inner)):
            target[part, o * height : (o + 1) * height] = value + more(part)

    def base_part(j, o):
        return lambda part: bases[j, part * size + o * height : part * size + (o + 1) * height]

    def finish_all(j, inner):
        whole = jnp.concatenate(left_of(j), 0)
        product = dot(whole, inner)
        step = 4 * height
        for o in range(OUTS):
            for part, value in enumerate(parts_of(product[o * step : (o + 1) * step])):
                g[j, part, o * height : (o + 1) * height] = value + base_part(j, o)(part)

    def give_turn():
        pl.semaphore_signal(turn, inc=1, device_id=(space, partner), device_id_type=MESH)

    @pl.when(space == 0)
    def _():
        if last > 1:
            settle()
        base = source(0)
        for j in range(1, slabs):
            g[j - 1, 0] = base[:size]
            g[j - 1, 1] = base[size:]
            if j < last:
                base = sandwich(step_lefts[j], step_rights[j], base) + source(j)
        wide = jnp.concatenate([base[:size], base[size:]], 1)
        inner = stacked(turned_block(rows_by(wide, step_rights[last])))
        if last < 2:
            settle()
        for o in range(OUTS):
            finish(
                made,
                o,
                step_lefts[last][o],
                inner,
                lambda part: src[last, part, o * height : (o + 1) * height],
            )
            if o == 0:
                enter()
            if stages > 1:
                @pl.when(first)
                def _():
                    send_on(o * CHUNKS // OUTS, CHUNKS // OUTS)
        if stages > 1 and paired:
            @pl.when(second)
            def _():
                pl.semaphore_wait(turn, 1)
                if stages > 2:
                    send_on(0, CHUNKS, True)
                else:
                    send_on(0, CHUNKS)
                give_turn()

            @pl.when(first)
            def _():
                sent(piece, 1)
                give_turn()
                pl.semaphore_wait(turn, 1)

        hear_all()
        spread(*range(last, -1, -1))

    @pl.when(space > 0)
    def _():
        settle()
        base = source(0)
        bases[0] = base
        for j in range(1, slabs):
            base = sandwich(step_lefts[j], step_rights[j], base) + source(j)
            bases[j] = base
        block = jnp.concatenate(coupler(0), 0)
        for j in range(slabs):
            if j > 0:
                block = columns_by(step_lefts[j], block)
            keep(j, block)

        @pl.when(gives | (hosted & (space == 1)))
        def _():
            own[0] = block
            own[1] = bases[last]
        enter()

        @pl.when(gives)
        def _():
            hand(space + 1, energy)

        if paired:
            @pl.when(hosted & (space == 1))
            def _():
                hand(space, partner)

        @pl.when(jnp.logical_not(odd & middle))
        def _():
            hear_all()

        @pl.when(takes)
        def _():
            ahead((own, early), space, energy).wait_recv()
            for j in range(slabs):
                left = left_of(j)
                bases[j] = sandwich(left, right_of(j), early[1]) + bases[j]
                block = columns_by(left, early[0])
                keep(j, block)
                if j == last:
                    @pl.when(hosted)
                    def _():
                        own[0] = block
                        own[1] = bases[last]

        if paired:
            @pl.when(hosted & (space > 1))
            def _():
                hand(space, partner)

        for c in range(GROUPS):
            line(made, entering, chain_recv, c * group, group, space, energy).wait_recv()
            lines = pl.ds(c * group, group)
            arrived = jnp.concatenate([entering[0, lines], entering[1, lines]], 1)
            if c < GROUPS - 1:
                for j in range(last, -1, -1):
                    spun[j, lines] = rows_by(arrived, right_of(j))

        def inner_of(j):
            tail = rows_by(arrived, right_of(j))
            return stacked(turned_block(jnp.concatenate([spun[j, : size - group], tail], 0)))

        @pl.when(stops)
        def _():
            inners = [inner_of(j) for j in range(slabs)]
            for j in range(last, -1, -1):
                finish_all(j, inners[j])
            spread(*range(last, -1, -1))

        @pl.when(jnp.logical_not(stops))
        def _():
            inner = inner_of(last)
            for o in range(OUTS):
                finish(made, o, lefts[last, o], inner, base_part(last, o))

                @pl.when(first)
                def _():
                    send_on(o * CHUNKS // OUTS, CHUNKS // OUTS)

        if paired:
            @pl.when(hosts)
            def _():
                ahead((own, early), space, energy).wait_recv()
                keep(slabs, early[0])
                turned = []
                for c in range(GROUPS):
                    line(made, guest, guest_recv, c * group, group, space, energy).wait_recv()
                    line(guest, entering, chain_recv, c * group, group, space, partner).start()
                    lines = pl.ds(c * group, group)
                    arrived = jnp.concatenate([guest[0, lines], guest[1, lines]], 1)
                    turned.append(rows_by(arrived, right_of(slabs)))
                inner = stacked(turned_block(jnp.concatenate(turned, 0)))
                for o in range(OUTS):
                    finish(
                        passed,
                        o,
                        lefts[slabs, o],
                        inner,
                        lambda part: early[
                            1, part * size + o * height : part * size + (o + 1) * height
                        ],
                    )
                    chunks = range(o * CHUNKS // OUTS, (o + 1) * CHUNKS // OUTS)

                    @pl.when(leaps & (space + 2 < stages - 1))
                    def _():
                        for c in chunks:
                            line(passed, guest, guest_recv, c * piece, piece, space + 2, energy).start()

                    @pl.when(leaps & (space + 2 == stages - 1))
                    def _():
                        for c in chunks:
                            line(
                                passed, entering, chain_recv, c * piece, piece, space + 2, partner
                            ).start()

                for c in range(CHUNKS):
                    line(passed, entering, chain_recv, c * piece, piece, space + 1, partner).start()
                give_turn()

            @pl.when(hosted)
            def _():
                pl.semaphore_wait(turn, 1)

        @pl.when(odd & middle)
        def _():
            hear_all()

        @pl.when(jnp.logical_not(stops))
        def _():
            spread(last)
            for j in range(last - 1, -1, -1):
                inner = inner_of(j)
                finish_all(j, inner)
                spread(j)

    def lanes(part):
        return pl.ds(part, rows, stride=2)

    loads[-1].wait()
    mine = pl.ds(pl.multiple_of(energy * rows, rows), rows)
    for j in range(last, -1, -1):
        landed[j, energy] = g[j, :, mine]
        others = landed.at[j, pl.ds(0, energies - 1)]
        pltpu.make_async_copy(others, others, swap_recv.at[j]).wait()
        for e in range(energies):
            real = jnp.zeros((rows, size), F32)
            imag = jnp.zeros((rows, size), F32)
            for w in range(e + 1):
                gr, gi = landed[j, e - w, 0], landed[j, e - w, 1]
                sr, si = scr[j, w, lanes(0)], scr[j, w, lanes(1)]
                real = real + (gr * sr - gi * si)
                imag = imag + (gr * si + gi * sr)
            out_se[j, e, lanes(0)] = real
            out_se[j, e, lanes(1)] = imag

    others = landed.at[:, pl.ds(0, energies - 1)]
    pltpu.make_async_copy(others, others, swap_send.at[0]).wait()

    @pl.when(gives | hosted)
    def _():
        ahead((own, early), space, energy).wait_send()

    @pl.when(first & (space < stages - 1))
    def _():
        sent(size - piece)
        if not paired:
            sent(piece, 1)

    if paired:
        @pl.when(first & middle)
        def _():
            sent(piece, 1)

        @pl.when(second & (space == 0) & (stages > 1))
        def _():
            if stages > 2:
                sent(size)
            else:
                sent(size - piece)
                sent(piece, 1)

        @pl.when(hosts)
        def _():
            sent(size)
            sent(size)

        @pl.when(leaps)
        def _():
            sent(size)


def write_out(g, se, out_g, out_se, sems):
    copies = [
        pltpu.make_async_copy(g, out_g.at[:, 0], sems.at[0]),
        pltpu.make_async_copy(se, out_se, sems.at[1]),
    ]
    for copy in copies:
        copy.start()
    for copy in copies:
        copy.wait()


def body(retain, hopping, source, screened):
    slabs, _, _, size, _ = hopping.shape
    energies = screened.shape[1]
    rows = screened.shape[3] // size
    woven = (
        screened.reshape(slabs, energies, 2, rows, size)
        .transpose(0, 1, 3, 2, 4)
        .reshape(slabs, energies, 2 * rows, size)
    )
    any_spec = pl.BlockSpec(memory_space=pl.ANY)
    vmem_spec = pl.BlockSpec(memory_space=pltpu.VMEM)
    vmem = pltpu.VMEM
    greens, self_energy = pl.pallas_call(
        kernel,
        out_shape=(vmem((slabs, 2, size, size), F32), vmem(woven.shape, F32)),
        in_specs=[pl.BlockSpec(memory_space=pltpu.HBM)] * 4,
        out_specs=(vmem_spec, vmem_spec),
        scratch_shapes=[
            pltpu.SMEM((slabs,), F32),
            vmem((2, slabs, 2, size, size), F32),
            vmem(woven.shape, F32),
            vmem((slabs + 1, OUTS, 4 * size // OUTS, 2 * size), BF16),
            vmem((slabs + 1, 2, 2 * size, 2 * size), BF16),
            vmem((slabs, 2 * size, size), F32),
            vmem((2, size, size), F32),
            vmem((slabs, energies, 2, rows, size), F32),
            vmem((2, 2 * size, size), F32),
            vmem((2, 2 * size, size), F32),
            vmem((2, size, size), F32),
            vmem((2, size, size), F32),
            vmem((slabs, size, 2 * size), F32),
            pltpu.SemaphoreType.DMA((4,)),
            pltpu.SemaphoreType.DMA((2,)),
            pltpu.SemaphoreType.DMA((GROUPS,)),
            pltpu.SemaphoreType.DMA((GROUPS,)),
            pltpu.SemaphoreType.DMA((1,)),
            pltpu.SemaphoreType.DMA((slabs,)),
            pltpu.SemaphoreType.DMA((2,)),
            pltpu.SemaphoreType.REGULAR,
            pltpu.SemaphoreType.REGULAR((max(energies.bit_length() - 2, 1),)),
        ],
        compiler_params=pltpu.CompilerParams(
            collective_id=0, has_side_effects=True
        ),
    )(retain.reshape(slabs), hopping, source, woven)
    greens, self_energy = pl.pallas_call(
        write_out,
        out_shape=(
            jax.ShapeDtypeStruct(source.shape, F32),
            jax.ShapeDtypeStruct(woven.shape, F32),
        ),
        in_specs=[vmem_spec, vmem_spec],
        out_specs=(any_spec, any_spec),
        scratch_shapes=[pltpu.SemaphoreType.DMA((2,))],
        compiler_params=pltpu.CompilerParams(vmem_limit_bytes=4 << 20),
    )(greens, self_energy)
    return greens, (
        self_energy.reshape(slabs, energies, rows, 2, size)
        .transpose(0, 1, 3, 2, 4)
        .reshape(screened.shape)
    )


def solution(mesh):
    placed = (
        P("space", "energy"),
        P("space", "energy", None, None, None),
        P("space", "energy", None, None, None),
        P("space", None, None, "energy"),
    )
    return jax.shard_map(
        body,
        mesh=mesh,
        in_specs=placed,
        out_specs=(P("space", "energy", None, None, None), P("space", None, None, "energy")),
        check_vma=False,
    )
```

```python
import functools

import jax
import jax.numpy as jnp
from jax import lax
from jax.experimental import pallas as pl
from jax.experimental.pallas import tpu as pltpu
from jax.sharding import PartitionSpec as P

MESH = pl.DeviceIdType.MESH
F32 = jnp.float32
BF16 = jnp.bfloat16
CHUNKS = 8
GROUPS = 4
OUTS = 4
ORDER = {6: 0, 7: 1, 4: 2, 5: 3, 2: 4, 3: 5, 1: 1 << 30}
LS = 4


def split(value):
    high = value.astype(BF16)
    return high, (value - high.astype(F32)).astype(BF16)


dot = functools.partial(
    lax.dot_general, dimension_numbers=(((1,), (0,)), ((), ())), preferred_element_type=F32
)


def rows_by(block, right):
    (high, low), (rh, rl) = split(block), right
    count = high.shape[0]
    both = dot(jnp.concatenate([high, low], 0), rh)
    return both[:count] + (dot(high, rl) + both[count:])


def left_form(real, imag):
    return jnp.concatenate(
        [jnp.concatenate([real, -imag], 1), jnp.concatenate([imag, real], 1)], 0
    )


def dagger_form(real, imag):
    real, imag = real.T, imag.T
    return jnp.concatenate(
        [jnp.concatenate([real, -imag], 1), jnp.concatenate([imag, real], 1)], 0
    )


def arranged(form):
    size = form.shape[0] // 2
    height = size // OUTS
    high, low = split(form)
    return [
        jnp.concatenate(
            [x[p * size + o * height : p * size + (o + 1) * height] for x in (high, low) for p in range(2)], 0
        )
        for o in range(OUTS)
    ]


def part_by(left, right):
    height, size = left.shape[0] // 4, right.shape[1] // 2
    product = dot(left[: 2 * height], right)
    other = dot(left[2 * height :], right[:, :size])
    both = product[:, :size] + (product[:, size:] + other)
    return both[:height], both[height:]


def parts_of(product):
    height, size = product.shape[0] // 4, product.shape[1] // 2
    cross = product[: 2 * height, size:] + product[2 * height :, :size]
    both = product[: 2 * height, :size] + cross
    return both[:height], both[height:]


def columns_by(left, block):
    right = stacked(block)
    parts = [part_by(x, right) for x in left]
    return jnp.concatenate([p[0] for p in parts] + [p[1] for p in parts], 0)


def stacked(block):
    return jnp.concatenate(split(block), 1)


def turned_block(turned):
    size = turned.shape[1] // 2
    return jnp.concatenate([turned[:, :size], turned[:, size:]], 0)


def kernel(
    retain_hbm, hop_hbm, src_hbm, scr_hbm, g, out_se,
    retain, slabs_in, scr, lefts, rights, bases, entering, landed, own, brought, early, guest, passed, spun,
    load_sem, chain_send, chain_recv, guest_recv, swap_send, swap_recv, ahead_sem, turn, ready,
):
    _, slabs, _, size, _ = slabs_in.shape
    energies, rows = landed.shape[1], landed.shape[3]
    space, energy = lax.axis_index("space"), lax.axis_index("energy")
    stages = lax.axis_size("space")
    piece, height, group = size // CHUNKS, size // OUTS, size // GROUPS
    last = slabs - 1
    paired = energies % 2 == 0
    power = energies & (energies - 1) == 0 and paired
    per = energies // OUTS
    quartered = power and per >= 2
    order = sorted(range(1, energies), key=lambda k: ORDER.get(k, k))
    hop, src = slabs_in.at[0], slabs_in.at[1]

    odd = lax.rem(space, 2) == 1
    middle = (space > 0) & (space < stages - 1)
    paired = paired and power
    if paired:
        partner = energy + 1 - 2 * lax.rem(energy, 2)
        second = lax.rem(energy, 2) == 0
    else:
        partner = energy
        second = energy < 0
    first = jnp.logical_not(second)
    hosts = first & (space > 0) & paired
    hosted = second & (space > 0)
    gives = second & middle & jnp.logical_not(odd)
    takes = hosts & odd & (space > 1)
    links = hosts & odd & middle
    leaps = links & (space + 2 < stages)

    loads = [
        pltpu.make_async_copy(retain_hbm, retain, load_sem.at[2]),
        *(
            pltpu.make_async_copy(
                array.at[which, 0, part, pl.ds(i * size // LS, size // LS)],
                ref.at[which, part, pl.ds(i * size // LS, size // LS)],
                load_sem.at[0],
            )
            for array, ref, which in (
                (hop_hbm, hop, slice(1, None)),
                (src_hbm, src, slice(0, 1)),
            )
            for part in range(2)
            for i in range(LS)
        ),
        pltpu.make_async_copy(src_hbm.at[1:, 0], src.at[1:], load_sem.at[3]),
        pltpu.make_async_copy(hop_hbm.at[:1, 0], hop.at[:1], load_sem.at[3]),
        pltpu.make_async_copy(scr_hbm, scr, load_sem.at[1]),
    ]
    for load in loads:
        load.start()

    barrier = pltpu.get_barrier_semaphore()

    def greet(where, who):
        pl.semaphore_signal(barrier, inc=1, device_id=(where, who), device_id_type=MESH)

    bits = [1 << b for b in range(energies.bit_length() - 1)] if power else []
    rounds = len(bits) - 1
    if power:
        for bit in bits:
            greet(space, jnp.bitwise_xor(energy, bit))
    else:
        for step in range(1, energies):
            greet(space, lax.rem(energy + step, energies))

    def call(level):
        if 0 < level <= rounds:
            for bit in bits:
                pl.semaphore_signal(
                    ready.at[level - 1],
                    inc=1,
                    device_id=(space, jnp.bitwise_xor(energy, bit)),
                    device_id_type=MESH,
                )

    def hear(level):
        if 0 < level <= rounds:
            pl.semaphore_wait(ready.at[level - 1], len(bits))
            call(level + 1)

    def hear_all():
        for level in range(1, rounds + 1):
            hear(level)

    @pl.when(first & (space > 0))
    def _():
        greet(space - 1, energy)

    if paired:
        @pl.when((hosts & (space == 1)) | takes)
        def _():
            greet(space - 1, partner)

        @pl.when(takes)
        def _():
            greet(space - 2, energy)

    greeted = (
        (len(bits) if power else energies - 1)
        + (first & (space < stages - 1)).astype(jnp.int32)
        + leaps.astype(jnp.int32)
        + (second & (space < stages - 1) & jnp.logical_not(odd)).astype(jnp.int32)
    )

    def enter():
        pl.semaphore_wait(barrier, greeted)
        call(1)

    loads[0].wait()
    pltpu.make_async_copy(hop, hop, load_sem.at[0]).wait()

    def settle():
        pltpu.make_async_copy(hop, hop, load_sem.at[3]).wait()

    eye = (
        lax.broadcasted_iota(jnp.int32, (size, size), 0)
        == lax.broadcasted_iota(jnp.int32, (size, size), 1)
    ).astype(F32)

    def coupler(j):
        factor = retain[j]
        return factor * (eye + hop[j, 0]), factor * hop[j, 1]

    def sandwich(left, right, block):
        wide = jnp.concatenate([block[:size], block[size:]], 1)
        return columns_by(left, turned_block(rows_by(wide, right)))

    def source(j):
        return jnp.concatenate([src[j, 0], src[j, 1]], 0)

    step_lefts, step_rights = [None], [None]
    for j in range(1, slabs):
        step_lefts.append(arranged(left_form(*coupler(j))))
        step_rights.append(split(dagger_form(*coupler(j))))

    def copy(source_ref, target_ref, sems, where, who):
        return pltpu.make_async_remote_copy(
            src_ref=source_ref,
            dst_ref=target_ref,
            send_sem=sems[0],
            recv_sem=sems[1],
            device_id=(where, who),
            device_id_type=MESH,
        )

    def line(source_ref, target_ref, recv, start, count, where, who, sem=0):
        lines = pl.ds(start, count)
        return copy(
            source_ref.at[:, lines],
            target_ref.at[:, lines],
            (chain_send.at[sem], recv.at[start // group]),
            where,
            who,
        )

    made = g.at[last]

    def send_on(begin, count, to_guest=False):
        for c in range(begin, begin + count):
            if to_guest:
                line(made, guest, guest_recv, c * piece, piece, space + 1, partner).start()
            else:
                line(made, entering, chain_recv, c * piece, piece, space + 1, energy, sem=int(c == 0)).start()

    def sent(count, sem=0):
        line(made, entering, chain_recv, 0, count, space, energy, sem=sem).wait_send()

    def ahead(where, who):
        return [
            copy(
                own.at[i * slabs + last], early.at[i], (ahead_sem.at[0], ahead_sem.at[1]), where, who
            )
            for i in range(2)
        ]

    def aheads():
        return copy(early, early, (ahead_sem.at[0], ahead_sem.at[1]), space, energy)

    def bring(refs=None):
        return copy(own, brought, (ahead_sem.at[0], ahead_sem.at[2]), space, partner)

    def swap(j, peer, source=None, who=None):
        rows_of = pl.ds(pl.multiple_of(peer * rows, rows), rows)
        return copy(
            (g if source is None else source).at[j, :, rows_of],
            landed.at[j, energy if who is None else who],
            (swap_send.at[0], swap_recv.at[j]),
            space,
            peer,
        )

    def spread_guest(*js):
        for k in order:
            if k > 1:
                peer = jnp.bitwise_xor(energy - lax.rem(energy, 2), k)
                for j in js:
                    swap(j, peer, passed, partner).start()

    def spread(*js):
        for k in order:
            if not power:
                peer = lax.rem(energy + k, energies)
            elif k == 1:
                peer = jnp.bitwise_xor(energy, 1)
            else:
                peer = jnp.bitwise_xor(energy - lax.rem(energy, 2), k)
            for j in js:
                swap(j, peer).start()

    def keep(j, block):
        real, imag = block[:size], block[size:]
        for o, part in enumerate(arranged(left_form(real, imag))):
            lefts[j, o] = part
        rights[j, 0], rights[j, 1] = split(dagger_form(real, imag))

    def left_of(j):
        return [lefts[j, o] for o in range(OUTS)]

    def right_of(j):
        return rights[j, 0], rights[j, 1]

    def finish(target, o, left, inner, more):
        for part, value in enumerate(part_by(left, inner)):
            target[part, o * height : (o + 1) * height] = value + more(part)

    def base_part(j, o):
        return lambda part: bases[j, part * size + o * height : part * size + (o + 1) * height]

    def finish_all(j, inner, target=None, more=None):
        whole = jnp.concatenate(left_of(j), 0)
        product = dot(whole, inner)
        step = 4 * height
        for o in range(OUTS):
            for part, value in enumerate(parts_of(product[o * step : (o + 1) * step])):
                start = part * size + o * height
                if target is None:
                    g[j, part, o * height : (o + 1) * height] = value + base_part(j, o)(part)
                else:
                    target[part, o * height : (o + 1) * height] = (
                        value + more[start : start + height]
                    )

    def give_turn():
        pl.semaphore_signal(turn, inc=1, device_id=(space, partner), device_id_type=MESH)

    @pl.when(space == 0)
    def _():
        if last > 1:
            settle()
        base = source(0)
        for j in range(1, slabs):
            g[j - 1, 0] = base[:size]
            g[j - 1, 1] = base[size:]
            if j < last:
                base = sandwich(step_lefts[j], step_rights[j], base) + source(j)
        wide = jnp.concatenate([base[:size], base[size:]], 1)
        inner = stacked(turned_block(rows_by(wide, step_rights[last])))
        if last < 2:
            settle()
        for o in range(OUTS):
            lines = slice(o * height, (o + 1) * height)
            finish(
                made,
                o,
                step_lefts[last][o],
                inner,
                lambda part: src[last, part, lines],
            )
            if o == 0:
                enter()
            if stages > 1:
                @pl.when(first)
                def _():
                    send_on(o * CHUNKS // OUTS, CHUNKS // OUTS)
        if stages > 1 and paired:
            @pl.when(second)
            def _():
                pl.semaphore_wait(turn, 1)
                send_on(0, CHUNKS, True)
                give_turn()

            @pl.when(first)
            def _():
                sent(piece, 1)
                give_turn()
                pl.semaphore_wait(turn, 1)

        hear_all()
        spread(*range(last, -1, -1))

    @pl.when(space > 0)
    def _():
        settle()
        base = source(0)
        bases[0] = base
        for j in range(1, slabs):
            base = sandwich(step_lefts[j], step_rights[j], base) + source(j)
            bases[j] = base
        block = jnp.concatenate(coupler(0), 0)
        for j in range(slabs):
            if j > 0:
                block = columns_by(step_lefts[j], block)
            keep(j, block)

            own[j] = block
            own[slabs + j] = bases[j]
        enter()

        if paired:
            @pl.when(hosted)
            def _():
                bring().start()

            @pl.when(gives)
            def _():
                for part in ahead(space + 1, partner):
                    part.start()

        @pl.when(hosted | jnp.logical_not(odd & middle))
        def _():
            hear_all()

        def gather(source_ref, recv, begin):
            for c in range(GROUPS):
                line(made, source_ref, recv, c * group, group, space, energy).wait_recv()
                if c < GROUPS - 1:
                    lines = pl.ds(c * group, group)
                    arrived = jnp.concatenate([source_ref[0, lines], source_ref[1, lines]], 1)
                    for j in range(last, -1, -1):
                        spun[begin + j, lines] = rows_by(arrived, right_of(begin + j))

        def inner_of(source_ref, begin, j):
            lines = pl.ds(size - group, group)
            arrived = jnp.concatenate([source_ref[0, lines], source_ref[1, lines]], 1)
            tail = rows_by(arrived, right_of(begin + j))
            return stacked(turned_block(jnp.concatenate([spun[begin + j, : size - group], tail], 0)))

        def own_part():
            gather(entering, chain_recv, 0)

            @pl.when(space == stages - 1)
            def _():
                inners = [inner_of(entering, 0, j) for j in range(slabs)]
                if quartered:
                    for d in range(OUTS - 1, -1, -1):
                        o = jnp.bitwise_xor(energy // per, d)
                        for j in range(last, -1, -1):
                            for part, value in enumerate(part_by(lefts[j, o], inners[j])):
                                at = pl.multiple_of(o * height, height)
                                g[j, part, pl.ds(at, height)] = (
                                    value + bases[j, pl.ds(part * size + at, height)]
                                )
                        for i in range(0 if d else 1, per):
                            peer = o * per + i if d else jnp.bitwise_xor(energy, i)
                            for j in range(last, -1, -1):
                                swap(j, peer).start()
                else:
                    for j in range(last, -1, -1):
                        finish_all(j, inners[j])
                    spread(*range(last, -1, -1))

            @pl.when(middle)
            def _():
                inner = inner_of(entering, 0, last)
                for o in range(OUTS):
                    finish(made, o, lefts[last, o], inner, base_part(last, o))
                    send_on(o * CHUNKS // OUTS, CHUNKS // OUTS)

        def own_rest():
            @pl.when(middle)
            def _():
                for j in range(last - 1, -1, -1):
                    finish_all(j, inner_of(entering, 0, j))

        def welcome():
            bring().wait_recv()
            for j in range(slabs):
                keep(slabs + j, brought[j])

        def guest_part():
            gather(guest, guest_recv, slabs)

            @pl.when(jnp.logical_not(odd & middle))
            def _():
                inners = [inner_of(guest, slabs, j) for j in range(slabs)]
                for j in range(last, -1, -1):
                    finish_all(slabs + j, inners[j], passed.at[j], brought.at[slabs + j])
                spread_guest(*range(last, -1, -1))
                copy(passed, g, (chain_send.at[0], chain_recv.at[0]), space, partner).start()

            @pl.when(odd & middle)
            def _():
                inner = inner_of(guest, slabs, last)
                out = passed.at[last]
                for o in range(OUTS):
                    finish(
                        out,
                        o,
                        lefts[slabs + last, o],
                        inner,
                        lambda part: brought[
                            slabs + last,
                            part * size + o * height : part * size + (o + 1) * height,
                        ],
                    )

                    @pl.when(leaps)
                    def _():
                        for c in range(o * CHUNKS // OUTS, (o + 1) * CHUNKS // OUTS):
                            line(out, guest, guest_recv, c * piece, piece, space + 2, energy).start()

                for c in range(CHUNKS):
                    line(out, guest, guest_recv, c * piece, piece, space + 1, energy).start()
                for j in range(last - 1, -1, -1):
                    finish_all(
                        slabs + j, inner_of(guest, slabs, j), passed.at[j], brought.at[slabs + j]
                    )
                copy(passed, g, (chain_send.at[0], chain_recv.at[0]), space, partner).start()

        if not paired:
            own_part()
            own_rest()
            @pl.when(middle)
            def _():
                spread(*range(last, -1, -1))
        else:
            @pl.when(takes)
            def _():
                welcome()
                aheads().wait_recv()
                for j in range(slabs):
                    left = left_of(slabs + j)
                    brought[slabs + j] = (
                        sandwich(left, right_of(slabs + j), early[1]) + brought[slabs + j]
                    )
                    keep(slabs + j, columns_by(left, early[0]))
                guest_part()

            @pl.when(first)
            def _():
                own_part()

            @pl.when(first & middle & jnp.logical_not(odd))
            def _():
                own_rest()
                spread(*range(last, -1, -1))

            @pl.when(hosts & jnp.logical_not(takes))
            def _():
                welcome()
                guest_part()

            @pl.when(links)
            def _():
                hear_all()
                spread(last)
                own_rest()
                spread(*range(last - 1, -1, -1))
                spread_guest(*range(last, -1, -1))

            @pl.when(hosts)
            def _():
                for j in range(slabs):
                    landed[j, partner] = passed[j, :, pl.ds(pl.multiple_of(energy * rows, rows), rows)]

            @pl.when(hosted)
            def _():
                copy(passed, g, (chain_send.at[0], chain_recv.at[0]), space, energy).wait_recv()

    def lanes(part):
        return pl.ds(part, rows, stride=2)

    loads[-1].wait()
    mine = pl.ds(pl.multiple_of(energy * rows, rows), rows)
    for j in range(last, -1, -1):
        landed[j, energy] = g[j, :, mine]
        for count, there in ((energies - 2, hosts), (energies - 1, jnp.logical_not(hosts))):
            @pl.when(there)
            def _():
                others = landed.at[j, pl.ds(0, count)]
                pltpu.make_async_copy(others, others, swap_recv.at[j]).wait()
        for e in range(energies):
            real = jnp.zeros((rows, size), F32)
            imag = jnp.zeros((rows, size), F32)
            for w in range(e + 1):
                gr, gi = landed[j, e - w, 0], landed[j, e - w, 1]
                sr, si = scr[j, w, lanes(0)], scr[j, w, lanes(1)]
                real = real + (gr * sr - gi * si)
                imag = imag + (gr * si + gi * sr)
            out_se[j, e, lanes(0)] = real
            out_se[j, e, lanes(1)] = imag

    others = landed.at[:, pl.ds(0, energies - 1)]
    fewer = landed.at[:, pl.ds(0, energies - 2)]

    @pl.when(jnp.logical_not(hosted))
    def _():
        pltpu.make_async_copy(others, others, swap_send.at[0]).wait()

    @pl.when(first & (space < stages - 1))
    def _():
        sent(size - piece)
        if not paired:
            sent(piece, 1)

    if paired:
        @pl.when(first & middle)
        def _():
            sent(piece, 1)

        @pl.when(hosted)
        def _():
            bring().wait_send()

        @pl.when(gives)
        def _():
            aheads().wait_send()

        @pl.when(second & (space == 0) & (stages > 1))
        def _():
            sent(size)

        @pl.when(hosts)
        def _():
            pltpu.make_async_copy(fewer, fewer, swap_send.at[0]).wait()
            copy(passed, g, (chain_send.at[0], chain_recv.at[0]), space, partner).wait_send()

        @pl.when(links)
        def _():
            sent(size)

        @pl.when(leaps)
        def _():
            sent(size)


def write_out(g, se, out_g, out_se, sems):
    copies = [
        pltpu.make_async_copy(g, out_g.at[:, 0], sems.at[0]),
        pltpu.make_async_copy(se, out_se, sems.at[1]),
    ]
    for copy in copies:
        copy.start()
    for copy in copies:
        copy.wait()


def body(retain, hopping, source, screened):
    slabs, _, _, size, _ = hopping.shape
    energies = screened.shape[1]
    rows = screened.shape[3] // size
    woven = (
        screened.reshape(slabs, energies, 2, rows, size)
        .transpose(0, 1, 3, 2, 4)
        .reshape(slabs, energies, 2 * rows, size)
    )
    any_spec = pl.BlockSpec(memory_space=pl.ANY)
    vmem_spec = pl.BlockSpec(memory_space=pltpu.VMEM)
    vmem = pltpu.VMEM
    greens, self_energy = pl.pallas_call(
        kernel,
        out_shape=(vmem((slabs, 2, size, size), F32), vmem(woven.shape, F32)),
        in_specs=[pl.BlockSpec(memory_space=pltpu.HBM)] * 4,
        out_specs=(vmem_spec, vmem_spec),
        scratch_shapes=[
            pltpu.SMEM((slabs,), F32),
            vmem((2, slabs, 2, size, size), F32),
            vmem(woven.shape, F32),
            vmem((2 * slabs, OUTS, 4 * size // OUTS, 2 * size), BF16),
            vmem((2 * slabs, 2, 2 * size, 2 * size), BF16),
            vmem((slabs, 2 * size, size), F32),
            vmem((2, size, size), F32),
            vmem((slabs, energies, 2, rows, size), F32),
            vmem((2 * slabs, 2 * size, size), F32),
            vmem((2 * slabs, 2 * size, size), F32),
            vmem((2, 2 * size, size), F32),
            vmem((2, size, size), F32),
            vmem((slabs, 2, size, size), F32),
            vmem((2 * slabs, size, 2 * size), F32),
            pltpu.SemaphoreType.DMA((4,)),
            pltpu.SemaphoreType.DMA((2,)),
            pltpu.SemaphoreType.DMA((GROUPS,)),
            pltpu.SemaphoreType.DMA((GROUPS,)),
            pltpu.SemaphoreType.DMA((1,)),
            pltpu.SemaphoreType.DMA((slabs,)),
            pltpu.SemaphoreType.DMA((3,)),
            pltpu.SemaphoreType.REGULAR,
            pltpu.SemaphoreType.REGULAR((max(energies.bit_length() - 2, 1),)),
        ],
        compiler_params=pltpu.CompilerParams(
            collective_id=0, has_side_effects=True
        ),
    )(retain.reshape(slabs), hopping, source, woven)
    greens, self_energy = pl.pallas_call(
        write_out,
        out_shape=(
            jax.ShapeDtypeStruct(source.shape, F32),
            jax.ShapeDtypeStruct(woven.shape, F32),
        ),
        in_specs=[vmem_spec, vmem_spec],
        out_specs=(any_spec, any_spec),
        scratch_shapes=[pltpu.SemaphoreType.DMA((2,))],
        compiler_params=pltpu.CompilerParams(vmem_limit_bytes=4 << 20),
    )(greens, self_energy)
    return greens, (
        self_energy.reshape(slabs, energies, rows, 2, size)
        .transpose(0, 1, 3, 2, 4)
        .reshape(screened.shape)
    )


def solution(mesh):
    placed = (
        P("space", "energy"),
        P("space", "energy", None, None, None),
        P("space", "energy", None, None, None),
        P("space", None, None, "energy"),
    )
    return jax.shard_map(
        body,
        mesh=mesh,
        in_specs=placed,
        out_specs=(P("space", "energy", None, None, None), P("space", None, None, "energy")),
        check_vma=False,
    )
```

```python
import functools

import jax
import jax.numpy as jnp
from jax import lax
from jax.experimental import pallas as pl
from jax.experimental.pallas import tpu as pltpu
from jax.sharding import PartitionSpec as P

MESH = pl.DeviceIdType.MESH
F32 = jnp.float32
BF16 = jnp.bfloat16
CHUNKS = 8
GROUPS = 4
OUTS = 4
ORDER = {6: 0, 7: 1, 4: 2, 5: 3, 2: 4, 3: 5, 1: 1 << 30}
LS = 4


def split(value):
    high = value.astype(BF16)
    return high, (value - high.astype(F32)).astype(BF16)


dot = functools.partial(
    lax.dot_general, dimension_numbers=(((1,), (0,)), ((), ())), preferred_element_type=F32
)


def rows_by(block, right):
    (high, low), (rh, rl) = split(block), right
    count = high.shape[0]
    both = dot(jnp.concatenate([high, low], 0), rh)
    return both[:count] + (dot(high, rl) + both[count:])


def left_form(real, imag):
    return jnp.concatenate(
        [jnp.concatenate([real, -imag], 1), jnp.concatenate([imag, real], 1)], 0
    )


def dagger_form(real, imag):
    real, imag = real.T, imag.T
    return jnp.concatenate(
        [jnp.concatenate([real, -imag], 1), jnp.concatenate([imag, real], 1)], 0
    )


def arranged(form):
    size = form.shape[0] // 2
    height = size // OUTS
    high, low = split(form)
    return [
        jnp.concatenate(
            [x[p * size + o * height : p * size + (o + 1) * height] for x in (high, low) for p in range(2)], 0
        )
        for o in range(OUTS)
    ]


def part_by(left, right):
    height, size = left.shape[0] // 4, right.shape[1] // 2
    product = dot(left[: 2 * height], right)
    other = dot(left[2 * height :], right[:, :size])
    both = product[:, :size] + (product[:, size:] + other)
    return both[:height], both[height:]


def parts_of(product):
    height, size = product.shape[0] // 4, product.shape[1] // 2
    cross = product[: 2 * height, size:] + product[2 * height :, :size]
    both = product[: 2 * height, :size] + cross
    return both[:height], both[height:]


def columns_by(left, block):
    right = stacked(block)
    parts = [part_by(x, right) for x in left]
    return jnp.concatenate([p[0] for p in parts] + [p[1] for p in parts], 0)


def stacked(block):
    return jnp.concatenate(split(block), 1)


def turned_block(turned):
    size = turned.shape[1] // 2
    return jnp.concatenate([turned[:, :size], turned[:, size:]], 0)


def kernel(
    retain_hbm, hop_hbm, src_hbm, scr_hbm, g, landed, scr,
    retain, slabs_in, lefts, rights, bases, entering, own, brought, early, guest, passed, spun,
    load_sem, chain_send, chain_recv, guest_recv, swap_send, swap_recv, ahead_sem, turn, ready,
):
    _, slabs, _, size, _ = slabs_in.shape
    energies, rows = landed.shape[1], landed.shape[3]
    space, energy = lax.axis_index("space"), lax.axis_index("energy")
    stages = lax.axis_size("space")
    piece, height, group = size // CHUNKS, size // OUTS, size // GROUPS
    last = slabs - 1
    paired = energies % 2 == 0
    power = energies & (energies - 1) == 0 and paired
    per = energies // OUTS
    quartered = power and per >= 2
    order = sorted(range(1, energies), key=lambda k: ORDER.get(k, k))
    hop, src = slabs_in.at[0], slabs_in.at[1]

    odd = lax.rem(space, 2) == 1
    middle = (space > 0) & (space < stages - 1)
    paired = paired and power
    if paired:
        partner = energy + 1 - 2 * lax.rem(energy, 2)
        second = lax.rem(energy, 2) == 0
    else:
        partner = energy
        second = energy < 0
    first = jnp.logical_not(second)
    hosts = first & (space > 0) & paired
    hosted = second & (space > 0)
    gives = second & middle & jnp.logical_not(odd)
    takes = hosts & odd & (space > 1)
    links = hosts & odd & middle
    leaps = links & (space + 2 < stages)

    loads = [
        pltpu.make_async_copy(retain_hbm, retain, load_sem.at[2]),
        *(
            pltpu.make_async_copy(
                array.at[which, 0, part, pl.ds(i * size // LS, size // LS)],
                ref.at[which, part, pl.ds(i * size // LS, size // LS)],
                load_sem.at[0],
            )
            for array, ref, which in (
                (hop_hbm, hop, slice(1, None)),
                (src_hbm, src, slice(0, 1)),
            )
            for part in range(2)
            for i in range(LS)
        ),
        pltpu.make_async_copy(src_hbm.at[1:, 0], src.at[1:], load_sem.at[3]),
        pltpu.make_async_copy(hop_hbm.at[:1, 0], hop.at[:1], load_sem.at[3]),
        pltpu.make_async_copy(scr_hbm, scr, load_sem.at[1]),
    ]
    for load in loads:
        load.start()

    barrier = pltpu.get_barrier_semaphore()

    def greet(where, who):
        pl.semaphore_signal(barrier, inc=1, device_id=(where, who), device_id_type=MESH)

    bits = [1 << b for b in range(energies.bit_length() - 1)] if power else []
    rounds = len(bits) - 1
    if power:
        for bit in bits:
            greet(space, jnp.bitwise_xor(energy, bit))
    else:
        for step in range(1, energies):
            greet(space, lax.rem(energy + step, energies))

    def call(level):
        if 0 < level <= rounds:
            for bit in bits:
                pl.semaphore_signal(
                    ready.at[level - 1],
                    inc=1,
                    device_id=(space, jnp.bitwise_xor(energy, bit)),
                    device_id_type=MESH,
                )

    def hear(level):
        if 0 < level <= rounds:
            pl.semaphore_wait(ready.at[level - 1], len(bits))
            call(level + 1)

    def hear_all():
        for level in range(1, rounds + 1):
            hear(level)

    @pl.when(first & (space > 0))
    def _():
        greet(space - 1, energy)

    if paired:
        @pl.when((hosts & (space == 1)) | takes)
        def _():
            greet(space - 1, partner)

        @pl.when(takes)
        def _():
            greet(space - 2, energy)

    greeted = (
        (len(bits) if power else energies - 1)
        + (first & (space < stages - 1)).astype(jnp.int32)
        + leaps.astype(jnp.int32)
        + (second & (space < stages - 1) & jnp.logical_not(odd)).astype(jnp.int32)
    )

    def enter():
        pl.semaphore_wait(barrier, greeted)
        call(1)

    loads[0].wait()
    pltpu.make_async_copy(hop, hop, load_sem.at[0]).wait()

    def settle():
        pltpu.make_async_copy(hop, hop, load_sem.at[3]).wait()

    eye = (
        lax.broadcasted_iota(jnp.int32, (size, size), 0)
        == lax.broadcasted_iota(jnp.int32, (size, size), 1)
    ).astype(F32)

    def coupler(j):
        factor = retain[j]
        return factor * (eye + hop[j, 0]), factor * hop[j, 1]

    def sandwich(left, right, block):
        wide = jnp.concatenate([block[:size], block[size:]], 1)
        return columns_by(left, turned_block(rows_by(wide, right)))

    def source(j):
        return jnp.concatenate([src[j, 0], src[j, 1]], 0)

    step_lefts, step_rights = [None], [None]
    for j in range(1, slabs):
        step_lefts.append(arranged(left_form(*coupler(j))))
        step_rights.append(split(dagger_form(*coupler(j))))

    def copy(source_ref, target_ref, sems, where, who):
        return pltpu.make_async_remote_copy(
            src_ref=source_ref,
            dst_ref=target_ref,
            send_sem=sems[0],
            recv_sem=sems[1],
            device_id=(where, who),
            device_id_type=MESH,
        )

    def line(source_ref, target_ref, recv, start, count, where, who, sem=0):
        lines = pl.ds(start, count)
        return copy(
            source_ref.at[:, lines],
            target_ref.at[:, lines],
            (chain_send.at[sem], recv.at[start // group]),
            where,
            who,
        )

    made = g.at[last]

    def send_on(begin, count, to_guest=False):
        for c in range(begin, begin + count):
            if to_guest:
                line(made, guest, guest_recv, c * piece, piece, space + 1, partner).start()
            else:
                line(made, entering, chain_recv, c * piece, piece, space + 1, energy, sem=int(c == 0)).start()

    def sent(count, sem=0):
        line(made, entering, chain_recv, 0, count, space, energy, sem=sem).wait_send()

    def ahead(i, where, who):
        return copy(
            own.at[i * slabs + last], early.at[i], (ahead_sem.at[0], ahead_sem.at[1]), where, who
        )

    def aheads():
        return copy(early, early, (ahead_sem.at[0], ahead_sem.at[1]), space, energy)

    def bring():
        return copy(own, brought, (ahead_sem.at[0], ahead_sem.at[2]), space, partner)

    def swap(j, peer, source=None, who=None):
        rows_of = pl.ds(pl.multiple_of(peer * rows, rows), rows)
        return copy(
            (g if source is None else source).at[j, :, rows_of],
            landed.at[j, energy if who is None else who],
            (swap_send.at[0], swap_recv.at[j]),
            space,
            peer,
        )

    def spread_guest(*js):
        for k in order:
            if k > 1:
                peer = jnp.bitwise_xor(energy - lax.rem(energy, 2), k)
                for j in js:
                    swap(j, peer, passed, partner).start()

    def spread(*js):
        for k in order:
            if not power:
                peer = lax.rem(energy + k, energies)
            elif k == 1:
                peer = jnp.bitwise_xor(energy, 1)
            else:
                peer = jnp.bitwise_xor(energy - lax.rem(energy, 2), k)
            for j in js:
                swap(j, peer).start()

    def keep(j, block):
        real, imag = block[:size], block[size:]
        for o, part in enumerate(arranged(left_form(real, imag))):
            lefts[j, o] = part
        rights[j, 0], rights[j, 1] = split(dagger_form(real, imag))

    def left_of(j):
        return [lefts[j, o] for o in range(OUTS)]

    def right_of(j):
        return rights[j, 0], rights[j, 1]

    def finish(target, o, left, inner, more):
        for part, value in enumerate(part_by(left, inner)):
            target[part, o * height : (o + 1) * height] = value + more(part)

    def base_part(j, o):
        return lambda part: bases[j, part * size + o * height : part * size + (o + 1) * height]

    def finish_all(j, inner, target=None, more=None):
        whole = jnp.concatenate(left_of(j), 0)
        product = dot(whole, inner)
        step = 4 * height
        for o in range(OUTS):
            for part, value in enumerate(parts_of(product[o * step : (o + 1) * step])):
                start = part * size + o * height
                if target is None:
                    g[j, part, o * height : (o + 1) * height] = value + base_part(j, o)(part)
                else:
                    target[part, o * height : (o + 1) * height] = (
                        value + more[start : start + height]
                    )

    def quarters(begin, inners, target, more, source_ref, who):
        for d in range(OUTS - 1, -1, -1):
            o = jnp.bitwise_xor(energy // per, d)
            at = pl.multiple_of(o * height, height)
            for j in range(last, -1, -1):
                for part, value in enumerate(part_by(lefts[begin + j, o], inners[j])):
                    target[j, part, pl.ds(at, height)] = (
                        value + more[begin + j, pl.ds(part * size + at, height)]
                    )
            if d:
                peers = [o * per + i for i in range(per)]
            else:
                peers = [jnp.bitwise_xor(energy, i) for i in range(2 if begin else 1, per)]
            for peer in peers:
                for j in range(last, -1, -1):
                    swap(j, peer, source_ref, who).start()

    def give_turn():
        pl.semaphore_signal(turn, inc=1, device_id=(space, partner), device_id_type=MESH)

    @pl.when(space == 0)
    def _():
        if last > 1:
            settle()
        base = source(0)
        for j in range(1, slabs):
            g[j - 1, 0] = base[:size]
            g[j - 1, 1] = base[size:]
            if j < last:
                base = sandwich(step_lefts[j], step_rights[j], base) + source(j)
        wide = jnp.concatenate([base[:size], base[size:]], 1)
        inner = stacked(turned_block(rows_by(wide, step_rights[last])))
        if last < 2:
            settle()
        for o in range(OUTS):
            lines = slice(o * height, (o + 1) * height)
            finish(
                made,
                o,
                step_lefts[last][o],
                inner,
                lambda part: src[last, part, lines],
            )
            if o == 0:
                enter()
            if stages > 1:
                @pl.when(first)
                def _():
                    send_on(o * CHUNKS // OUTS, CHUNKS // OUTS)
        if stages > 1 and paired:
            @pl.when(second)
            def _():
                pl.semaphore_wait(turn, 1)
                send_on(0, CHUNKS, True)
                give_turn()

            @pl.when(first)
            def _():
                sent(piece, 1)
                give_turn()
                pl.semaphore_wait(turn, 1)

        hear_all()
        spread(*range(last, -1, -1))

    @pl.when(space > 0)
    def _():
        settle()
        block = jnp.concatenate(coupler(0), 0)
        for j in range(slabs):
            if j > 0:
                block = columns_by(step_lefts[j], block)
            keep(j, block)
            own[j] = block
        enter()

        if paired:
            @pl.when(gives)
            def _():
                ahead(0, space + 1, partner).start()

        base = source(0)
        bases[0] = base
        own[slabs] = base
        for j in range(1, slabs):
            base = sandwich(step_lefts[j], step_rights[j], base) + source(j)
            bases[j] = base
            own[slabs + j] = base
        if paired:
            @pl.when(gives)
            def _():
                ahead(1, space + 1, partner).start()

            @pl.when(hosted)
            def _():
                bring().start()

        @pl.when(hosted | jnp.logical_not(odd & middle))
        def _():
            hear_all()

        def gather(source_ref, recv, begin):
            for c in range(GROUPS):
                line(made, source_ref, recv, c * group, group, space, energy).wait_recv()
                if c < GROUPS - 1:
                    lines = pl.ds(c * group, group)
                    arrived = jnp.concatenate([source_ref[0, lines], source_ref[1, lines]], 1)
                    for j in range(last, -1, -1):
                        spun[begin + j, lines] = rows_by(arrived, right_of(begin + j))

        def inner_of(source_ref, begin, j):
            lines = pl.ds(size - group, group)
            arrived = jnp.concatenate([source_ref[0, lines], source_ref[1, lines]], 1)
            tail = rows_by(arrived, right_of(begin + j))
            return stacked(turned_block(jnp.concatenate([spun[begin + j, : size - group], tail], 0)))

        def own_part():
            gather(entering, chain_recv, 0)

            @pl.when(space == stages - 1)
            def _():
                inners = [inner_of(entering, 0, j) for j in range(slabs)]
                if quartered:
                    quarters(0, inners, g, bases, None, None)
                else:
                    for j in range(last, -1, -1):
                        finish_all(j, inners[j])
                    spread(*range(last, -1, -1))

            @pl.when(middle)
            def _():
                inner = inner_of(entering, 0, last)
                for o in range(OUTS):
                    finish(made, o, lefts[last, o], inner, base_part(last, o))
                    send_on(o * CHUNKS // OUTS, CHUNKS // OUTS)

        def own_rest():
            @pl.when(middle)
            def _():
                for j in range(last - 1, -1, -1):
                    finish_all(j, inner_of(entering, 0, j))

        def welcome():
            bring().wait_recv()
            for j in range(slabs):
                keep(slabs + j, brought[j])

        def guest_part():
            gather(guest, guest_recv, slabs)

            @pl.when(jnp.logical_not(odd & middle))
            def _():
                inners = [inner_of(guest, slabs, j) for j in range(slabs)]
                if quartered:
                    quarters(slabs, inners, passed, brought, passed, partner)
                else:
                    for j in range(last, -1, -1):
                        finish_all(slabs + j, inners[j], passed.at[j], brought.at[slabs + j])
                    spread_guest(*range(last, -1, -1))
                copy(passed, g, (chain_send.at[0], chain_recv.at[0]), space, partner).start()

            @pl.when(odd & middle)
            def _():
                inner = inner_of(guest, slabs, last)
                out = passed.at[last]
                for o in range(OUTS):
                    finish(
                        out,
                        o,
                        lefts[slabs + last, o],
                        inner,
                        lambda part: brought[
                            slabs + last,
                            part * size + o * height : part * size + (o + 1) * height,
                        ],
                    )

                    @pl.when(leaps)
                    def _():
                        for c in range(o * CHUNKS // OUTS, (o + 1) * CHUNKS // OUTS):
                            line(out, guest, guest_recv, c * piece, piece, space + 2, energy).start()

                for c in range(CHUNKS):
                    line(out, guest, guest_recv, c * piece, piece, space + 1, energy).start()
                for j in range(last - 1, -1, -1):
                    finish_all(
                        slabs + j, inner_of(guest, slabs, j), passed.at[j], brought.at[slabs + j]
                    )
                copy(passed, g, (chain_send.at[0], chain_recv.at[0]), space, partner).start()

        if not paired:
            own_part()
            own_rest()
            @pl.when(middle)
            def _():
                spread(*range(last, -1, -1))
        else:
            @pl.when(takes)
            def _():
                welcome()
                aheads().wait_recv()
                for j in range(slabs):
                    left = left_of(slabs + j)
                    brought[slabs + j] = (
                        sandwich(left, right_of(slabs + j), early[1]) + brought[slabs + j]
                    )
                    keep(slabs + j, columns_by(left, early[0]))
                guest_part()

            @pl.when(first)
            def _():
                own_part()

            @pl.when(first & middle & jnp.logical_not(odd))
            def _():
                own_rest()
                spread(*range(last, -1, -1))

            @pl.when(hosts & jnp.logical_not(takes))
            def _():
                welcome()
                guest_part()

            @pl.when(links)
            def _():
                hear_all()
                spread(last)
                own_rest()
                spread(*range(last - 1, -1, -1))
                spread_guest(*range(last, -1, -1))

            @pl.when(hosts)
            def _():
                for j in range(slabs):
                    landed[j, partner] = passed[j, :, pl.ds(pl.multiple_of(energy * rows, rows), rows)]

            @pl.when(hosted)
            def _():
                copy(passed, g, (chain_send.at[0], chain_recv.at[0]), space, energy).wait_recv()

    loads[-1].wait()
    mine = pl.ds(pl.multiple_of(energy * rows, rows), rows)
    for j in range(last, -1, -1):
        landed[j, energy] = g[j, :, mine]
        for count, there in ((energies - 2, hosts), (energies - 1, jnp.logical_not(hosts))):
            @pl.when(there)
            def _():
                others = landed.at[j, pl.ds(0, count)]
                pltpu.make_async_copy(others, others, swap_recv.at[j]).wait()

    others = landed.at[:, pl.ds(0, energies - 1)]
    fewer = landed.at[:, pl.ds(0, energies - 2)]

    @pl.when(jnp.logical_not(hosted))
    def _():
        pltpu.make_async_copy(others, others, swap_send.at[0]).wait()

    @pl.when(first & (space < stages - 1))
    def _():
        sent(size - piece)
        if not paired:
            sent(piece, 1)

    if paired:
        @pl.when(first & middle)
        def _():
            sent(piece, 1)

        @pl.when(hosted)
        def _():
            bring().wait_send()

        @pl.when(gives)
        def _():
            aheads().wait_send()

        @pl.when(second & (space == 0) & (stages > 1))
        def _():
            sent(size)

        @pl.when(hosts)
        def _():
            pltpu.make_async_copy(fewer, fewer, swap_send.at[0]).wait()
            copy(passed, g, (chain_send.at[0], chain_recv.at[0]), space, partner).wait_send()

        @pl.when(links)
        def _():
            sent(size)

        @pl.when(leaps)
        def _():
            sent(size)


def write_out(g, landed, scr, out_g, out_se, se, sems):
    slabs, energies, _, rows, size = landed.shape

    def lanes(part):
        return pl.ds(part, rows, stride=2)

    pltpu.make_async_copy(g, out_g.at[:, 0], sems.at[0]).start()
    for j in range(slabs):
        for e in range(energies):
            real = jnp.zeros((rows, size), F32)
            imag = jnp.zeros((rows, size), F32)
            for w in range(e + 1):
                gr, gi = landed[j, e - w, 0], landed[j, e - w, 1]
                sr, si = scr[j, w, lanes(0)], scr[j, w, lanes(1)]
                real = real + (gr * sr - gi * si)
                imag = imag + (gr * si + gi * sr)
            se[j, e, lanes(0)] = real
            se[j, e, lanes(1)] = imag
        pltpu.make_async_copy(se.at[j], out_se.at[j], sems.at[1]).start()
    pltpu.make_async_copy(g, out_g.at[:, 0], sems.at[0]).wait()
    pltpu.make_async_copy(se, out_se, sems.at[1]).wait()


def body(retain, hopping, source, screened):
    slabs, _, _, size, _ = hopping.shape
    energies = screened.shape[1]
    rows = screened.shape[3] // size
    woven = (
        screened.reshape(slabs, energies, 2, rows, size)
        .transpose(0, 1, 3, 2, 4)
        .reshape(slabs, energies, 2 * rows, size)
    )
    any_spec = pl.BlockSpec(memory_space=pl.ANY)
    vmem_spec = pl.BlockSpec(memory_space=pltpu.VMEM)
    vmem = pltpu.VMEM
    greens, landed, kept = pl.pallas_call(
        kernel,
        out_shape=(
            vmem((slabs, 2, size, size), F32),
            vmem((slabs, energies, 2, rows, size), F32),
            vmem(woven.shape, F32),
        ),
        in_specs=[pl.BlockSpec(memory_space=pltpu.HBM)] * 4,
        out_specs=(vmem_spec,) * 3,
        scratch_shapes=[
            pltpu.SMEM((slabs,), F32),
            vmem((2, slabs, 2, size, size), F32),
            vmem((2 * slabs, OUTS, 4 * size // OUTS, 2 * size), BF16),
            vmem((2 * slabs, 2, 2 * size, 2 * size), BF16),
            vmem((slabs, 2 * size, size), F32),
            vmem((2, size, size), F32),
            vmem((2 * slabs, 2 * size, size), F32),
            vmem((2 * slabs, 2 * size, size), F32),
            vmem((2, 2 * size, size), F32),
            vmem((2, size, size), F32),
            vmem((slabs, 2, size, size), F32),
            vmem((2 * slabs, size, 2 * size), F32),
            pltpu.SemaphoreType.DMA((4,)),
            pltpu.SemaphoreType.DMA((2,)),
            pltpu.SemaphoreType.DMA((GROUPS,)),
            pltpu.SemaphoreType.DMA((GROUPS,)),
            pltpu.SemaphoreType.DMA((1,)),
            pltpu.SemaphoreType.DMA((slabs,)),
            pltpu.SemaphoreType.DMA((3,)),
            pltpu.SemaphoreType.REGULAR,
            pltpu.SemaphoreType.REGULAR((max(energies.bit_length() - 2, 1),)),
        ],
        compiler_params=pltpu.CompilerParams(
            collective_id=0, has_side_effects=True
        ),
    )(retain.reshape(slabs), hopping, source, woven)
    greens, self_energy = pl.pallas_call(
        write_out,
        out_shape=(
            jax.ShapeDtypeStruct(source.shape, F32),
            jax.ShapeDtypeStruct(woven.shape, F32),
        ),
        in_specs=[vmem_spec] * 3,
        out_specs=(any_spec, any_spec),
        scratch_shapes=[vmem(woven.shape, F32), pltpu.SemaphoreType.DMA((2,))],
        compiler_params=pltpu.CompilerParams(vmem_limit_bytes=4 << 20),
    )(greens, landed, kept)
    return greens, (
        self_energy.reshape(slabs, energies, rows, 2, size)
        .transpose(0, 1, 3, 2, 4)
        .reshape(screened.shape)
    )


def solution(mesh):
    placed = (
        P("space", "energy"),
        P("space", "energy", None, None, None),
        P("space", "energy", None, None, None),
        P("space", None, None, "energy"),
    )
    return jax.shard_map(
        body,
        mesh=mesh,
        in_specs=placed,
        out_specs=(P("space", "energy", None, None, None), P("space", None, None, "energy")),
        check_vma=False,
    )
```

```python
import functools

import jax
import jax.numpy as jnp
from jax import lax
from jax.experimental import pallas as pl
from jax.experimental.pallas import tpu as pltpu
from jax.sharding import PartitionSpec as P

MESH = pl.DeviceIdType.MESH
F32 = jnp.float32
BF16 = jnp.bfloat16
CHUNKS = 8
GROUPS = 4
OUTS = 4
ORDER = {6: 0, 7: 1, 4: 2, 5: 3, 2: 4, 3: 5, 1: 1 << 30}
LS = 4


def split(value):
    high = value.astype(BF16)
    return high, (value - high.astype(F32)).astype(BF16)


dot = functools.partial(
    lax.dot_general, dimension_numbers=(((1,), (0,)), ((), ())), preferred_element_type=F32
)


def rows_by(block, right):
    (high, low), (rh, rl) = split(block), right
    count = high.shape[0]
    both = dot(jnp.concatenate([high, low], 0), rh)
    return both[:count] + (dot(high, rl) + both[count:])


def left_form(real, imag):
    return jnp.concatenate(
        [jnp.concatenate([real, -imag], 1), jnp.concatenate([imag, real], 1)], 0
    )


def dagger_form(real, imag):
    real, imag = real.T, imag.T
    return jnp.concatenate(
        [jnp.concatenate([real, -imag], 1), jnp.concatenate([imag, real], 1)], 0
    )


def arranged(form):
    size = form.shape[0] // 2
    height = size // OUTS
    high, low = split(form)
    return [
        jnp.concatenate(
            [x[p * size + o * height : p * size + (o + 1) * height] for x in (high, low) for p in range(2)], 0
        )
        for o in range(OUTS)
    ]


def part_by(left, right):
    height, size = left.shape[0] // 4, right.shape[1] // 2
    product = dot(left[: 2 * height], right)
    other = dot(left[2 * height :], right[:, :size])
    both = product[:, :size] + (product[:, size:] + other)
    return both[:height], both[height:]


def parts_of(product):
    height, size = product.shape[0] // 4, product.shape[1] // 2
    cross = product[: 2 * height, size:] + product[2 * height :, :size]
    both = product[: 2 * height, :size] + cross
    return both[:height], both[height:]


def columns_by(left, block):
    right = stacked(block)
    parts = [part_by(x, right) for x in left]
    return jnp.concatenate([p[0] for p in parts] + [p[1] for p in parts], 0)


def stacked(block):
    return jnp.concatenate(split(block), 1)


def turned_block(turned):
    size = turned.shape[1] // 2
    return jnp.concatenate([turned[:, :size], turned[:, size:]], 0)


def kernel(
    retain_hbm, hop_hbm, src_hbm, scr_hbm, g, landed, scr,
    retain, slabs_in, lefts, rights, bases, entering, own, brought, early, guest, passed, spun,
    load_sem, chain_send, chain_recv, guest_recv, swap_send, swap_recv, ahead_sem, turn, ready,
):
    _, slabs, _, size, _ = slabs_in.shape
    energies, rows = landed.shape[1], landed.shape[3]
    space, energy = lax.axis_index("space"), lax.axis_index("energy")
    stages = lax.axis_size("space")
    piece, height, group = size // CHUNKS, size // OUTS, size // GROUPS
    last = slabs - 1
    paired = energies % 2 == 0
    power = energies & (energies - 1) == 0 and paired
    per = energies // OUTS
    quartered = power and per >= 2
    order = sorted(range(1, energies), key=lambda k: ORDER.get(k, k))
    hop, src = slabs_in.at[0], slabs_in.at[1]

    odd = lax.rem(space, 2) == 1
    middle = (space > 0) & (space < stages - 1)
    paired = paired and power
    if paired:
        partner = energy + 1 - 2 * lax.rem(energy, 2)
        second = lax.rem(energy, 2) == 0
    else:
        partner = energy
        second = energy < 0
    first = jnp.logical_not(second)
    hosts = first & (space > 0) & paired
    hosted = second & (space > 0)
    gives = second & middle & jnp.logical_not(odd)
    takes = hosts & odd & (space > 1)
    links = hosts & odd & middle
    leaps = links & (space + 2 < stages)

    loads = [
        pltpu.make_async_copy(retain_hbm, retain, load_sem.at[2]),
        *(
            pltpu.make_async_copy(
                array.at[which, 0, part, pl.ds(i * size // LS, size // LS)],
                ref.at[which, part, pl.ds(i * size // LS, size // LS)],
                load_sem.at[0],
            )
            for array, ref, which in (
                (hop_hbm, hop, slice(1, None)),
                (src_hbm, src, slice(0, 1)),
            )
            for part in range(2)
            for i in range(LS)
        ),
        pltpu.make_async_copy(src_hbm.at[1:, 0], src.at[1:], load_sem.at[3]),
        pltpu.make_async_copy(hop_hbm.at[:1, 0], hop.at[:1], load_sem.at[3]),
        pltpu.make_async_copy(scr_hbm, scr, load_sem.at[1]),
    ]
    for load in loads:
        load.start()

    barrier = pltpu.get_barrier_semaphore()

    def greet(where, who):
        pl.semaphore_signal(barrier, inc=1, device_id=(where, who), device_id_type=MESH)

    bits = [1 << b for b in range(energies.bit_length() - 1)] if power else []
    rounds = len(bits) - 1
    if power:
        for bit in bits:
            greet(space, jnp.bitwise_xor(energy, bit))
    else:
        for step in range(1, energies):
            greet(space, lax.rem(energy + step, energies))

    def call(level):
        if 0 < level <= rounds:
            for bit in bits:
                pl.semaphore_signal(
                    ready.at[level - 1],
                    inc=1,
                    device_id=(space, jnp.bitwise_xor(energy, bit)),
                    device_id_type=MESH,
                )

    def hear(level):
        if 0 < level <= rounds:
            pl.semaphore_wait(ready.at[level - 1], len(bits))
            call(level + 1)

    def hear_all():
        for level in range(1, rounds + 1):
            hear(level)

    @pl.when(first & (space > 0))
    def _():
        greet(space - 1, energy)

    if paired:
        @pl.when((hosts & (space == 1)) | takes)
        def _():
            greet(space - 1, partner)

        @pl.when(takes)
        def _():
            greet(space - 2, energy)

    greeted = (
        (len(bits) if power else energies - 1)
        + (first & (space < stages - 1)).astype(jnp.int32)
        + leaps.astype(jnp.int32)
        + (second & (space < stages - 1) & jnp.logical_not(odd)).astype(jnp.int32)
    )

    def enter():
        pl.semaphore_wait(barrier, greeted)
        call(1)

    loads[0].wait()
    pltpu.make_async_copy(hop, hop, load_sem.at[0]).wait()

    def settle():
        pltpu.make_async_copy(hop, hop, load_sem.at[3]).wait()

    eye = (
        lax.broadcasted_iota(jnp.int32, (size, size), 0)
        == lax.broadcasted_iota(jnp.int32, (size, size), 1)
    ).astype(F32)

    def coupler(j):
        factor = retain[j]
        return factor * (eye + hop[j, 0]), factor * hop[j, 1]

    def sandwich(left, right, block):
        wide = jnp.concatenate([block[:size], block[size:]], 1)
        return columns_by(left, turned_block(rows_by(wide, right)))

    def source(j):
        return jnp.concatenate([src[j, 0], src[j, 1]], 0)

    step_lefts, step_rights = [None], [None]
    for j in range(1, slabs):
        step_lefts.append(arranged(left_form(*coupler(j))))
        step_rights.append(split(dagger_form(*coupler(j))))

    def copy(source_ref, target_ref, sems, where, who):
        return pltpu.make_async_remote_copy(
            src_ref=source_ref,
            dst_ref=target_ref,
            send_sem=sems[0],
            recv_sem=sems[1],
            device_id=(where, who),
            device_id_type=MESH,
        )

    def line(source_ref, target_ref, recv, start, count, where, who, sem=0):
        lines = pl.ds(start, count)
        return copy(
            source_ref.at[:, lines],
            target_ref.at[:, lines],
            (chain_send.at[sem], recv.at[start // group]),
            where,
            who,
        )

    made = g.at[last]

    def send_on(begin, count, to_guest=False):
        for c in range(begin, begin + count):
            if to_guest:
                line(made, guest, guest_recv, c * piece, piece, space + 1, partner).start()
            else:
                line(made, entering, chain_recv, c * piece, piece, space + 1, energy, sem=int(c == 0)).start()

    def sent(count, sem=0):
        line(made, entering, chain_recv, 0, count, space, energy, sem=sem).wait_send()

    def ahead(i, where, who):
        return copy(
            own.at[i * slabs + last], early.at[i], (ahead_sem.at[0], ahead_sem.at[1]), where, who
        )

    def aheads():
        return copy(early, early, (ahead_sem.at[0], ahead_sem.at[1]), space, energy)

    def bring():
        return copy(own, brought, (ahead_sem.at[0], ahead_sem.at[2]), space, partner)

    def swap(j, peer, source=None, who=None):
        rows_of = pl.ds(pl.multiple_of(peer * rows, rows), rows)
        return copy(
            (g if source is None else source).at[j, :, rows_of],
            landed.at[j, energy if who is None else who],
            (swap_send.at[0], swap_recv.at[j]),
            space,
            peer,
        )

    def spread_guest(*js):
        for k in order:
            if k > 1:
                peer = jnp.bitwise_xor(energy - lax.rem(energy, 2), k)
                for j in js:
                    swap(j, peer, passed, partner).start()

    def spread(*js):
        for k in order:
            if not power:
                peer = lax.rem(energy + k, energies)
            elif k == 1:
                peer = jnp.bitwise_xor(energy, 1)
            else:
                peer = jnp.bitwise_xor(energy - lax.rem(energy, 2), k)
            for j in js:
                swap(j, peer).start()

    def keep(j, block):
        real, imag = block[:size], block[size:]
        for o, part in enumerate(arranged(left_form(real, imag))):
            lefts[j, o] = part
        rights[j, 0], rights[j, 1] = split(dagger_form(real, imag))

    def left_of(j):
        return [lefts[j, o] for o in range(OUTS)]

    def right_of(j):
        return rights[j, 0], rights[j, 1]

    def finish(target, o, left, inner, more):
        for part, value in enumerate(part_by(left, inner)):
            target[part, o * height : (o + 1) * height] = value + more(part)

    def base_part(j, o):
        return lambda part: bases[j, part * size + o * height : part * size + (o + 1) * height]

    def finish_all(j, inner, target=None, more=None):
        whole = jnp.concatenate(left_of(j), 0)
        product = dot(whole, inner)
        step = 4 * height
        for o in range(OUTS):
            for part, value in enumerate(parts_of(product[o * step : (o + 1) * step])):
                start = part * size + o * height
                if target is None:
                    g[j, part, o * height : (o + 1) * height] = value + base_part(j, o)(part)
                else:
                    target[part, o * height : (o + 1) * height] = (
                        value + more[start : start + height]
                    )

    def quarters(begin, inners, target, more, source_ref, who):
        for d in range(OUTS - 1, -1, -1):
            o = jnp.bitwise_xor(energy // per, d)
            at = pl.multiple_of(o * height, height)
            for j in range(last, -1, -1):
                for part, value in enumerate(part_by(lefts[begin + j, o], inners[j])):
                    target[j, part, pl.ds(at, height)] = (
                        value + more[begin + j, pl.ds(part * size + at, height)]
                    )
            if d:
                peers = [o * per + i for i in range(per)]
            else:
                peers = [jnp.bitwise_xor(energy, i) for i in range(2 if begin else 1, per)]
            for peer in peers:
                for j in range(last, -1, -1):
                    swap(j, peer, source_ref, who).start()

    def give_turn():
        pl.semaphore_signal(turn, inc=1, device_id=(space, partner), device_id_type=MESH)

    @pl.when(space == 0)
    def _():
        if last > 1:
            settle()
        base = source(0)
        for j in range(1, slabs):
            g[j - 1, 0] = base[:size]
            g[j - 1, 1] = base[size:]
            if j < last:
                base = sandwich(step_lefts[j], step_rights[j], base) + source(j)
        wide = jnp.concatenate([base[:size], base[size:]], 1)
        inner = stacked(turned_block(rows_by(wide, step_rights[last])))
        if last < 2:
            settle()
        for o in range(OUTS):
            lines = slice(o * height, (o + 1) * height)
            finish(
                made,
                o,
                step_lefts[last][o],
                inner,
                lambda part: src[last, part, lines],
            )
            if o == 0:
                enter()
            if stages > 1:
                @pl.when(first)
                def _():
                    send_on(o * CHUNKS // OUTS, CHUNKS // OUTS)
        if stages > 1 and paired:
            @pl.when(second)
            def _():
                pl.semaphore_wait(turn, 1)
                send_on(0, CHUNKS, True)
                give_turn()

            @pl.when(first)
            def _():
                sent(piece, 1)
                give_turn()
                pl.semaphore_wait(turn, 1)

        hear_all()
        spread(*range(last, -1, -1))

    @pl.when(space > 0)
    def _():
        settle()
        block = jnp.concatenate(coupler(0), 0)
        for j in range(slabs):
            if j > 0:
                block = columns_by(step_lefts[j], block)
            keep(j, block)
            own[j] = block
        enter()

        if paired:
            @pl.when(gives)
            def _():
                ahead(0, space + 1, partner).start()

        base = source(0)
        bases[0] = base
        own[slabs] = base
        for j in range(1, slabs):
            base = sandwich(step_lefts[j], step_rights[j], base) + source(j)
            bases[j] = base
            own[slabs + j] = base
        if paired:
            @pl.when(gives)
            def _():
                ahead(1, space + 1, partner).start()

            @pl.when(hosted)
            def _():
                bring().start()

        @pl.when(hosted | jnp.logical_not(odd & middle))
        def _():
            hear_all()

        def gather(source_ref, recv, begin):
            for c in range(GROUPS):
                line(made, source_ref, recv, c * group, group, space, energy).wait_recv()
                if c < GROUPS - 1:
                    lines = pl.ds(c * group, group)
                    arrived = jnp.concatenate([source_ref[0, lines], source_ref[1, lines]], 1)
                    for j in range(last, -1, -1):
                        spun[begin + j, lines] = rows_by(arrived, right_of(begin + j))

        def inner_of(source_ref, begin, j):
            lines = pl.ds(size - group, group)
            arrived = jnp.concatenate([source_ref[0, lines], source_ref[1, lines]], 1)
            tail = rows_by(arrived, right_of(begin + j))
            return stacked(turned_block(jnp.concatenate([spun[begin + j, : size - group], tail], 0)))

        def own_part():
            gather(entering, chain_recv, 0)

            @pl.when(space == stages - 1)
            def _():
                inners = [inner_of(entering, 0, j) for j in range(slabs)]
                if quartered:
                    quarters(0, inners, g, bases, None, None)
                else:
                    for j in range(last, -1, -1):
                        finish_all(j, inners[j])
                    spread(*range(last, -1, -1))

            @pl.when(middle)
            def _():
                inner = inner_of(entering, 0, last)
                for o in range(OUTS):
                    finish(made, o, lefts[last, o], inner, base_part(last, o))
                    send_on(o * CHUNKS // OUTS, CHUNKS // OUTS)

        def own_rest():
            @pl.when(middle)
            def _():
                for j in range(last - 1, -1, -1):
                    finish_all(j, inner_of(entering, 0, j))

        def welcome():
            bring().wait_recv()
            for j in range(slabs):
                keep(slabs + j, brought[j])

        def guest_part():
            gather(guest, guest_recv, slabs)

            @pl.when(jnp.logical_not(odd & middle))
            def _():
                inners = [inner_of(guest, slabs, j) for j in range(slabs)]
                if quartered:
                    quarters(slabs, inners, passed, brought, passed, partner)
                else:
                    for j in range(last, -1, -1):
                        finish_all(slabs + j, inners[j], passed.at[j], brought.at[slabs + j])
                    spread_guest(*range(last, -1, -1))
                copy(passed, g, (chain_send.at[0], chain_recv.at[0]), space, partner).start()

            @pl.when(odd & middle)
            def _():
                inner = inner_of(guest, slabs, last)
                out = passed.at[last]
                for o in range(OUTS):
                    finish(
                        out,
                        o,
                        lefts[slabs + last, o],
                        inner,
                        lambda part: brought[
                            slabs + last,
                            part * size + o * height : part * size + (o + 1) * height,
                        ],
                    )

                    @pl.when(leaps)
                    def _():
                        for c in range(o * CHUNKS // OUTS, (o + 1) * CHUNKS // OUTS):
                            line(out, guest, guest_recv, c * piece, piece, space + 2, energy).start()

                for c in range(CHUNKS):
                    line(out, guest, guest_recv, c * piece, piece, space + 1, energy).start()
                for j in range(last - 1, -1, -1):
                    finish_all(
                        slabs + j, inner_of(guest, slabs, j), passed.at[j], brought.at[slabs + j]
                    )
                copy(passed, g, (chain_send.at[0], chain_recv.at[0]), space, partner).start()

        if not paired:
            own_part()
            own_rest()
            @pl.when(middle)
            def _():
                spread(*range(last, -1, -1))
        else:
            @pl.when(takes)
            def _():
                welcome()
                aheads().wait_recv()
                for j in range(slabs):
                    left = left_of(slabs + j)
                    brought[slabs + j] = (
                        sandwich(left, right_of(slabs + j), early[1]) + brought[slabs + j]
                    )
                    keep(slabs + j, columns_by(left, early[0]))
                guest_part()

            @pl.when(first)
            def _():
                own_part()

            @pl.when(first & middle & jnp.logical_not(odd))
            def _():
                own_rest()
                spread(*range(last, -1, -1))

            @pl.when(hosts & jnp.logical_not(takes))
            def _():
                welcome()
                guest_part()

            @pl.when(links)
            def _():
                hear_all()
                spread(last)
                own_rest()
                spread(*range(last - 1, -1, -1))
                spread_guest(*range(last, -1, -1))

            @pl.when(hosts)
            def _():
                for j in range(slabs):
                    landed[j, partner] = passed[j, :, pl.ds(pl.multiple_of(energy * rows, rows), rows)]

            @pl.when(hosted)
            def _():
                copy(passed, g, (chain_send.at[0], chain_recv.at[0]), space, energy).wait_recv()

    loads[-1].wait()
    mine = pl.ds(pl.multiple_of(energy * rows, rows), rows)
    for j in range(last, -1, -1):
        landed[j, energy] = g[j, :, mine]
        for count, there in ((energies - 2, hosts), (energies - 1, jnp.logical_not(hosts))):
            @pl.when(there)
            def _():
                others = landed.at[j, pl.ds(0, count)]
                pltpu.make_async_copy(others, others, swap_recv.at[j]).wait()

    others = landed.at[:, pl.ds(0, energies - 1)]
    fewer = landed.at[:, pl.ds(0, energies - 2)]

    @pl.when(jnp.logical_not(hosted))
    def _():
        pltpu.make_async_copy(others, others, swap_send.at[0]).wait()

    @pl.when(first & (space < stages - 1))
    def _():
        sent(size - piece)
        if not paired:
            sent(piece, 1)

    if paired:
        @pl.when(first & middle)
        def _():
            sent(piece, 1)

        @pl.when(hosted)
        def _():
            bring().wait_send()

        @pl.when(gives)
        def _():
            aheads().wait_send()

        @pl.when(second & (space == 0) & (stages > 1))
        def _():
            sent(size)

        @pl.when(hosts)
        def _():
            pltpu.make_async_copy(fewer, fewer, swap_send.at[0]).wait()
            copy(passed, g, (chain_send.at[0], chain_recv.at[0]), space, partner).wait_send()

        @pl.when(links)
        def _():
            sent(size)

        @pl.when(leaps)
        def _():
            sent(size)


def write_out(g, landed, scr, out_g, out_se, se, sems):
    slabs, energies, _, rows, size = landed.shape
    span = energies // 4 if energies % 4 == 0 else energies

    def lanes(part):
        return pl.ds(part, rows, stride=2)

    pltpu.make_async_copy(g, out_g.at[:, 0], sems.at[0]).start()
    for j in range(slabs):
        for e in range(energies):
            real = jnp.zeros((rows, size), F32)
            imag = jnp.zeros((rows, size), F32)
            for w in range(e + 1):
                gr, gi = landed[j, e - w, 0], landed[j, e - w, 1]
                sr, si = scr[j, w, lanes(0)], scr[j, w, lanes(1)]
                real = real + (gr * sr - gi * si)
                imag = imag + (gr * si + gi * sr)
            se[j, e, lanes(0)] = real
            se[j, e, lanes(1)] = imag
            if (e + 1) % span == 0:
                part = pl.ds(e + 1 - span, span)
                pltpu.make_async_copy(se.at[j, part], out_se.at[j, part], sems.at[1]).start()
    pltpu.make_async_copy(g, out_g.at[:, 0], sems.at[0]).wait()
    pltpu.make_async_copy(se, out_se, sems.at[1]).wait()


def body(retain, hopping, source, screened):
    slabs, _, _, size, _ = hopping.shape
    energies = screened.shape[1]
    rows = screened.shape[3] // size
    woven = (
        screened.reshape(slabs, energies, 2, rows, size)
        .transpose(0, 1, 3, 2, 4)
        .reshape(slabs, energies, 2 * rows, size)
    )
    any_spec = pl.BlockSpec(memory_space=pl.ANY)
    vmem_spec = pl.BlockSpec(memory_space=pltpu.VMEM)
    vmem = pltpu.VMEM
    greens, landed, kept = pl.pallas_call(
        kernel,
        out_shape=(
            vmem((slabs, 2, size, size), F32),
            vmem((slabs, energies, 2, rows, size), F32),
            vmem(woven.shape, F32),
        ),
        in_specs=[pl.BlockSpec(memory_space=pltpu.HBM)] * 4,
        out_specs=(vmem_spec,) * 3,
        scratch_shapes=[
            pltpu.SMEM((slabs,), F32),
            vmem((2, slabs, 2, size, size), F32),
            vmem((2 * slabs, OUTS, 4 * size // OUTS, 2 * size), BF16),
            vmem((2 * slabs, 2, 2 * size, 2 * size), BF16),
            vmem((slabs, 2 * size, size), F32),
            vmem((2, size, size), F32),
            vmem((2 * slabs, 2 * size, size), F32),
            vmem((2 * slabs, 2 * size, size), F32),
            vmem((2, 2 * size, size), F32),
            vmem((2, size, size), F32),
            vmem((slabs, 2, size, size), F32),
            vmem((2 * slabs, size, 2 * size), F32),
            pltpu.SemaphoreType.DMA((4,)),
            pltpu.SemaphoreType.DMA((2,)),
            pltpu.SemaphoreType.DMA((GROUPS,)),
            pltpu.SemaphoreType.DMA((GROUPS,)),
            pltpu.SemaphoreType.DMA((1,)),
            pltpu.SemaphoreType.DMA((slabs,)),
            pltpu.SemaphoreType.DMA((3,)),
            pltpu.SemaphoreType.REGULAR,
            pltpu.SemaphoreType.REGULAR((max(energies.bit_length() - 2, 1),)),
        ],
        compiler_params=pltpu.CompilerParams(
            collective_id=0, has_side_effects=True
        ),
    )(retain.reshape(slabs), hopping, source, woven)
    greens, self_energy = pl.pallas_call(
        write_out,
        out_shape=(
            jax.ShapeDtypeStruct(source.shape, F32),
            jax.ShapeDtypeStruct(woven.shape, F32),
        ),
        in_specs=[vmem_spec] * 3,
        out_specs=(any_spec, any_spec),
        scratch_shapes=[vmem(woven.shape, F32), pltpu.SemaphoreType.DMA((2,))],
        compiler_params=pltpu.CompilerParams(vmem_limit_bytes=4 << 20),
    )(greens, landed, kept)
    return greens, (
        self_energy.reshape(slabs, energies, rows, 2, size)
        .transpose(0, 1, 3, 2, 4)
        .reshape(screened.shape)
    )


def solution(mesh):
    placed = (
        P("space", "energy"),
        P("space", "energy", None, None, None),
        P("space", "energy", None, None, None),
        P("space", None, None, "energy"),
    )
    return jax.shard_map(
        body,
        mesh=mesh,
        in_specs=placed,
        out_specs=(P("space", "energy", None, None, None), P("space", None, None, "energy")),
        check_vma=False,
    )
```

```python
import functools

import jax
import jax.numpy as jnp
from jax import lax
from jax.experimental import pallas as pl
from jax.experimental.pallas import tpu as pltpu
from jax.sharding import PartitionSpec as P

MESH = pl.DeviceIdType.MESH
F32 = jnp.float32
BF16 = jnp.bfloat16
CHUNKS = 8
GROUPS = 4
OUTS = 4
ORDER = {6: 0, 7: 1, 4: 2, 5: 3, 2: 4, 3: 5, 1: 1 << 30}
LS = 4


def split(value):
    high = value.astype(BF16)
    return high, (value - high.astype(F32)).astype(BF16)


dot = functools.partial(
    lax.dot_general, dimension_numbers=(((1,), (0,)), ((), ())), preferred_element_type=F32
)


def rows_by(block, right):
    (high, low), (rh, rl) = split(block), right
    count = high.shape[0]
    both = dot(jnp.concatenate([high, low], 0), rh)
    return both[:count] + (dot(high, rl) + both[count:])


def left_form(real, imag):
    return jnp.concatenate(
        [jnp.concatenate([real, -imag], 1), jnp.concatenate([imag, real], 1)], 0
    )


def dagger_form(real, imag):
    real, imag = real.T, imag.T
    return jnp.concatenate(
        [jnp.concatenate([real, -imag], 1), jnp.concatenate([imag, real], 1)], 0
    )


def arranged(form):
    size = form.shape[0] // 2
    height = size // OUTS
    high, low = split(form)
    return [
        jnp.concatenate(
            [x[p * size + o * height : p * size + (o + 1) * height] for x in (high, low) for p in range(2)], 0
        )
        for o in range(OUTS)
    ]


def part_by(left, right):
    height, size = left.shape[0] // 4, right.shape[1] // 2
    product = dot(left[: 2 * height], right)
    other = dot(left[2 * height :], right[:, :size])
    both = product[:, :size] + (product[:, size:] + other)
    return both[:height], both[height:]


def parts_of(product):
    height, size = product.shape[0] // 4, product.shape[1] // 2
    cross = product[: 2 * height, size:] + product[2 * height :, :size]
    both = product[: 2 * height, :size] + cross
    return both[:height], both[height:]


def columns_by(left, block):
    right = stacked(block)
    parts = [part_by(x, right) for x in left]
    return jnp.concatenate([p[0] for p in parts] + [p[1] for p in parts], 0)


def stacked(block):
    return jnp.concatenate(split(block), 1)


def turned_block(turned):
    size = turned.shape[1] // 2
    return jnp.concatenate([turned[:, :size], turned[:, size:]], 0)


def kernel(
    retain_hbm, hop_hbm, src_hbm, scr_hbm, g, landed, scr,
    retain, slabs_in, lefts, rights, bases, entering, own, brought, early, guest, passed, spun,
    load_sem, chain_send, chain_recv, guest_recv, swap_send, swap_recv, ahead_sem, turn, ready,
):
    _, slabs, _, size, _ = slabs_in.shape
    energies, rows = landed.shape[1], landed.shape[3]
    space, energy = lax.axis_index("space"), lax.axis_index("energy")
    stages = lax.axis_size("space")
    piece, height, group = size // CHUNKS, size // OUTS, size // GROUPS
    last = slabs - 1
    paired = energies % 2 == 0
    power = energies & (energies - 1) == 0 and paired
    per = energies // OUTS
    quartered = power and per >= 2
    order = sorted(range(1, energies), key=lambda k: ORDER.get(k, k))
    hop, src = slabs_in.at[0], slabs_in.at[1]

    odd = lax.rem(space, 2) == 1
    middle = (space > 0) & (space < stages - 1)
    paired = paired and power
    if paired:
        partner = energy + 1 - 2 * lax.rem(energy, 2)
        second = lax.rem(energy, 2) == 0
    else:
        partner = energy
        second = energy < 0
    first = jnp.logical_not(second)
    hosts = first & (space > 0) & paired
    hosted = second & (space > 0)
    gives = second & middle & jnp.logical_not(odd)
    takes = hosts & odd & (space > 1)
    links = hosts & odd & middle
    leaps = links & (space + 2 < stages)

    loads = [
        pltpu.make_async_copy(retain_hbm, retain, swap_send.at[0]),
        *(
            pltpu.make_async_copy(
                array.at[which, 0, part, pl.ds(i * size // LS, size // LS)],
                ref.at[which, part, pl.ds(i * size // LS, size // LS)],
                chain_send.at[0],
            )
            for array, ref, which in (
                (hop_hbm, hop, slice(1, None)),
                (src_hbm, src, slice(0, 1)),
            )
            for part in range(2)
            for i in range(LS)
        ),
        pltpu.make_async_copy(src_hbm.at[1:, 0], src.at[1:], chain_send.at[1]),
        pltpu.make_async_copy(hop_hbm.at[:1, 0], hop.at[:1], chain_send.at[1]),
        pltpu.make_async_copy(scr_hbm, scr, load_sem.at[0]),
    ]
    for load in loads:
        load.start()

    barrier = pltpu.get_barrier_semaphore()

    def greet(where, who):
        pl.semaphore_signal(barrier, inc=1, device_id=(where, who), device_id_type=MESH)

    bits = [1 << b for b in range(energies.bit_length() - 1)] if power else []
    rounds = len(bits) - 1
    if power:
        for bit in bits:
            greet(space, jnp.bitwise_xor(energy, bit))
    else:
        for step in range(1, energies):
            greet(space, lax.rem(energy + step, energies))

    def call(level):
        if 0 < level <= rounds:
            for bit in bits:
                pl.semaphore_signal(
                    ready.at[level - 1],
                    inc=1,
                    device_id=(space, jnp.bitwise_xor(energy, bit)),
                    device_id_type=MESH,
                )

    def hear(level):
        if 0 < level <= rounds:
            pl.semaphore_wait(ready.at[level - 1], len(bits))
            call(level + 1)

    def hear_all():
        for level in range(1, rounds + 1):
            hear(level)

    @pl.when(first & (space > 0))
    def _():
        greet(space - 1, energy)

    if paired:
        @pl.when((hosts & (space == 1)) | takes)
        def _():
            greet(space - 1, partner)

        @pl.when(takes)
        def _():
            greet(space - 2, energy)

    greeted = (
        (len(bits) if power else energies - 1)
        + (first & (space < stages - 1)).astype(jnp.int32)
        + leaps.astype(jnp.int32)
        + (second & (space < stages - 1) & jnp.logical_not(odd)).astype(jnp.int32)
    )

    def enter():
        pl.semaphore_wait(barrier, greeted)
        call(1)

    loads[0].wait()
    pltpu.make_async_copy(hop, hop, chain_send.at[0]).wait()

    def settle():
        pltpu.make_async_copy(hop, hop, chain_send.at[1]).wait()

    eye = (
        lax.broadcasted_iota(jnp.int32, (size, size), 0)
        == lax.broadcasted_iota(jnp.int32, (size, size), 1)
    ).astype(F32)

    def coupler(j):
        factor = retain[j]
        return factor * (eye + hop[j, 0]), factor * hop[j, 1]

    def sandwich(left, right, block):
        wide = jnp.concatenate([block[:size], block[size:]], 1)
        return columns_by(left, turned_block(rows_by(wide, right)))

    def source(j):
        return jnp.concatenate([src[j, 0], src[j, 1]], 0)

    step_lefts, step_rights = [None], [None]
    for j in range(1, slabs):
        step_lefts.append(arranged(left_form(*coupler(j))))
        step_rights.append(split(dagger_form(*coupler(j))))

    def copy(source_ref, target_ref, sems, where, who):
        return pltpu.make_async_remote_copy(
            src_ref=source_ref,
            dst_ref=target_ref,
            send_sem=sems[0],
            recv_sem=sems[1],
            device_id=(where, who),
            device_id_type=MESH,
        )

    def line(source_ref, target_ref, recv, start, count, where, who, sem=0):
        lines = pl.ds(start, count)
        return copy(
            source_ref.at[:, lines],
            target_ref.at[:, lines],
            (chain_send.at[sem], recv.at[start // group]),
            where,
            who,
        )

    made = g.at[last]

    def send_on(begin, count, to_guest=False):
        for c in range(begin, begin + count):
            if to_guest:
                line(made, guest, guest_recv, c * piece, piece, space + 1, partner).start()
            else:
                line(made, entering, chain_recv, c * piece, piece, space + 1, energy, sem=int(c == 0)).start()

    def sent(count, sem=0):
        line(made, entering, chain_recv, 0, count, space, energy, sem=sem).wait_send()

    def ahead(i, where, who):
        return copy(
            own.at[i * slabs + last], early.at[i], (ahead_sem.at[0], ahead_sem.at[1]), where, who
        )

    def aheads():
        return copy(early, early, (ahead_sem.at[0], ahead_sem.at[1]), space, energy)

    def bring():
        return copy(own, brought, (ahead_sem.at[0], ahead_sem.at[2]), space, partner)

    def swap(j, peer, source=None, who=None):
        rows_of = pl.ds(pl.multiple_of(peer * rows, rows), rows)
        return copy(
            (g if source is None else source).at[j, :, rows_of],
            landed.at[j, energy if who is None else who],
            (swap_send.at[0], swap_recv.at[j]),
            space,
            peer,
        )

    def spread_guest(*js):
        for k in order:
            if k > 1:
                peer = jnp.bitwise_xor(energy - lax.rem(energy, 2), k)
                for j in js:
                    swap(j, peer, passed, partner).start()

    def spread(*js):
        for k in order:
            if not power:
                peer = lax.rem(energy + k, energies)
            elif k == 1:
                peer = jnp.bitwise_xor(energy, 1)
            else:
                peer = jnp.bitwise_xor(energy - lax.rem(energy, 2), k)
            for j in js:
                swap(j, peer).start()

    def keep(j, block):
        real, imag = block[:size], block[size:]
        for o, part in enumerate(arranged(left_form(real, imag))):
            lefts[j, o] = part
        rights[j, 0], rights[j, 1] = split(dagger_form(real, imag))

    def left_of(j):
        return [lefts[j, o] for o in range(OUTS)]

    def right_of(j):
        return rights[j, 0], rights[j, 1]

    def finish(target, o, left, inner, more):
        for part, value in enumerate(part_by(left, inner)):
            target[part, o * height : (o + 1) * height] = value + more(part)

    def base_part(j, o):
        return lambda part: bases[j, part * size + o * height : part * size + (o + 1) * height]

    def finish_all(j, inner, target=None, more=None):
        whole = jnp.concatenate(left_of(j), 0)
        product = dot(whole, inner)
        step = 4 * height
        for o in range(OUTS):
            for part, value in enumerate(parts_of(product[o * step : (o + 1) * step])):
                start = part * size + o * height
                if target is None:
                    g[j, part, o * height : (o + 1) * height] = value + base_part(j, o)(part)
                else:
                    target[part, o * height : (o + 1) * height] = (
                        value + more[start : start + height]
                    )

    def quarters(begin, inners, target, more, source_ref, who):
        for d in range(OUTS - 1, -1, -1):
            o = jnp.bitwise_xor(energy // per, d)
            at = pl.multiple_of(o * height, height)
            for j in range(last, -1, -1):
                for part, value in enumerate(part_by(lefts[begin + j, o], inners[j])):
                    target[j, part, pl.ds(at, height)] = (
                        value + more[begin + j, pl.ds(part * size + at, height)]
                    )
            if d:
                peers = [o * per + i for i in range(per)]
            else:
                peers = [jnp.bitwise_xor(energy, i) for i in range(2 if begin else 1, per)]
            for peer in peers:
                for j in range(last, -1, -1):
                    swap(j, peer, source_ref, who).start()

    def give_turn():
        pl.semaphore_signal(turn, inc=1, device_id=(space, partner), device_id_type=MESH)

    @pl.when(space == 0)
    def _():
        if last > 1:
            settle()
        base = source(0)
        for j in range(1, slabs):
            g[j - 1, 0] = base[:size]
            g[j - 1, 1] = base[size:]
            if j < last:
                base = sandwich(step_lefts[j], step_rights[j], base) + source(j)
        wide = jnp.concatenate([base[:size], base[size:]], 1)
        inner = stacked(turned_block(rows_by(wide, step_rights[last])))
        if last < 2:
            settle()
        for o in range(OUTS):
            lines = slice(o * height, (o + 1) * height)
            finish(
                made,
                o,
                step_lefts[last][o],
                inner,
                lambda part: src[last, part, lines],
            )
            if o == 0:
                enter()
            if stages > 1:
                @pl.when(first)
                def _():
                    send_on(o * CHUNKS // OUTS, CHUNKS // OUTS)
        if stages > 1 and paired:
            @pl.when(second)
            def _():
                pl.semaphore_wait(turn, 1)
                send_on(0, CHUNKS, True)
                give_turn()

            @pl.when(first)
            def _():
                sent(piece, 1)
                give_turn()
                pl.semaphore_wait(turn, 1)

        hear_all()
        spread(*range(last, -1, -1))

    @pl.when(space > 0)
    def _():
        settle()
        block = jnp.concatenate(coupler(0), 0)
        for j in range(slabs):
            if j > 0:
                block = columns_by(step_lefts[j], block)
            keep(j, block)
            own[j] = block
        enter()

        if paired:
            @pl.when(gives)
            def _():
                ahead(0, space + 1, partner).start()

        base = source(0)
        bases[0] = base
        own[slabs] = base
        for j in range(1, slabs):
            base = sandwich(step_lefts[j], step_rights[j], base) + source(j)
            bases[j] = base
            own[slabs + j] = base
        if paired:
            @pl.when(gives)
            def _():
                ahead(1, space + 1, partner).start()

            @pl.when(hosted)
            def _():
                bring().start()

        @pl.when(hosted | jnp.logical_not(odd & middle))
        def _():
            hear_all()

        def gather(source_ref, recv, begin):
            for c in range(GROUPS):
                line(made, source_ref, recv, c * group, group, space, energy).wait_recv()
                if c < GROUPS - 1:
                    lines = pl.ds(c * group, group)
                    arrived = jnp.concatenate([source_ref[0, lines], source_ref[1, lines]], 1)
                    for j in range(last, -1, -1):
                        spun[begin + j, lines] = rows_by(arrived, right_of(begin + j))

        def inner_of(source_ref, begin, j):
            lines = pl.ds(size - group, group)
            arrived = jnp.concatenate([source_ref[0, lines], source_ref[1, lines]], 1)
            tail = rows_by(arrived, right_of(begin + j))
            return stacked(turned_block(jnp.concatenate([spun[begin + j, : size - group], tail], 0)))

        def own_part():
            gather(entering, chain_recv, 0)

            @pl.when(space == stages - 1)
            def _():
                inners = [inner_of(entering, 0, j) for j in range(slabs)]
                if quartered:
                    quarters(0, inners, g, bases, None, None)
                else:
                    for j in range(last, -1, -1):
                        finish_all(j, inners[j])
                    spread(*range(last, -1, -1))

            @pl.when(middle)
            def _():
                inner = inner_of(entering, 0, last)
                for o in range(OUTS):
                    finish(made, o, lefts[last, o], inner, base_part(last, o))
                    send_on(o * CHUNKS // OUTS, CHUNKS // OUTS)

        def own_rest():
            @pl.when(middle)
            def _():
                for j in range(last - 1, -1, -1):
                    finish_all(j, inner_of(entering, 0, j))

        def welcome():
            bring().wait_recv()
            for j in range(slabs):
                keep(slabs + j, brought[j])

        def guest_part():
            gather(guest, guest_recv, slabs)

            @pl.when(jnp.logical_not(odd & middle))
            def _():
                inners = [inner_of(guest, slabs, j) for j in range(slabs)]
                if quartered:
                    quarters(slabs, inners, passed, brought, passed, partner)
                else:
                    for j in range(last, -1, -1):
                        finish_all(slabs + j, inners[j], passed.at[j], brought.at[slabs + j])
                    spread_guest(*range(last, -1, -1))
                copy(passed, g, (chain_send.at[0], chain_recv.at[0]), space, partner).start()

            @pl.when(odd & middle)
            def _():
                inner = inner_of(guest, slabs, last)
                out = passed.at[last]
                for o in range(OUTS):
                    finish(
                        out,
                        o,
                        lefts[slabs + last, o],
                        inner,
                        lambda part: brought[
                            slabs + last,
                            part * size + o * height : part * size + (o + 1) * height,
                        ],
                    )

                    @pl.when(leaps)
                    def _():
                        for c in range(o * CHUNKS // OUTS, (o + 1) * CHUNKS // OUTS):
                            line(out, guest, guest_recv, c * piece, piece, space + 2, energy).start()

                for c in range(CHUNKS):
                    line(out, guest, guest_recv, c * piece, piece, space + 1, energy).start()
                for j in range(last - 1, -1, -1):
                    finish_all(
                        slabs + j, inner_of(guest, slabs, j), passed.at[j], brought.at[slabs + j]
                    )
                copy(passed, g, (chain_send.at[0], chain_recv.at[0]), space, partner).start()

        if not paired:
            own_part()
            own_rest()
            @pl.when(middle)
            def _():
                spread(*range(last, -1, -1))
        else:
            @pl.when(takes)
            def _():
                welcome()
                aheads().wait_recv()
                for j in range(slabs):
                    left = left_of(slabs + j)
                    brought[slabs + j] = (
                        sandwich(left, right_of(slabs + j), early[1]) + brought[slabs + j]
                    )
                    keep(slabs + j, columns_by(left, early[0]))
                guest_part()

            @pl.when(first)
            def _():
                own_part()

            @pl.when(first & middle & jnp.logical_not(odd))
            def _():
                own_rest()
                spread(*range(last, -1, -1))

            @pl.when(hosts & jnp.logical_not(takes))
            def _():
                welcome()
                guest_part()

            @pl.when(links)
            def _():
                hear_all()
                spread(last)
                own_rest()
                spread(*range(last - 1, -1, -1))
                spread_guest(*range(last, -1, -1))

            @pl.when(hosts)
            def _():
                for j in range(slabs):
                    landed[j, partner] = passed[j, :, pl.ds(pl.multiple_of(energy * rows, rows), rows)]

            @pl.when(hosted)
            def _():
                copy(passed, g, (chain_send.at[0], chain_recv.at[0]), space, energy).wait_recv()

    loads[-1].wait()
    mine = pl.ds(pl.multiple_of(energy * rows, rows), rows)
    for j in range(last, -1, -1):
        landed[j, energy] = g[j, :, mine]
        for count, there in ((energies - 2, hosts), (energies - 1, jnp.logical_not(hosts))):
            @pl.when(there)
            def _():
                others = landed.at[j, pl.ds(0, count)]
                pltpu.make_async_copy(others, others, swap_recv.at[j]).wait()

    others = landed.at[:, pl.ds(0, energies - 1)]
    fewer = landed.at[:, pl.ds(0, energies - 2)]

    @pl.when(jnp.logical_not(hosted))
    def _():
        pltpu.make_async_copy(others, others, swap_send.at[0]).wait()

    @pl.when(first & (space < stages - 1))
    def _():
        sent(size - piece)
        if not paired:
            sent(piece, 1)

    if paired:
        @pl.when(first & middle)
        def _():
            sent(piece, 1)

        @pl.when(hosted)
        def _():
            bring().wait_send()

        @pl.when(gives)
        def _():
            aheads().wait_send()

        @pl.when(second & (space == 0) & (stages > 1))
        def _():
            sent(size)

        @pl.when(hosts)
        def _():
            pltpu.make_async_copy(fewer, fewer, swap_send.at[0]).wait()
            copy(passed, g, (chain_send.at[0], chain_recv.at[0]), space, partner).wait_send()

        @pl.when(links)
        def _():
            sent(size)

        @pl.when(leaps)
        def _():
            sent(size)


def write_out(g, landed, scr, out_g, out_se, se, sems):
    slabs, energies, _, rows, size = landed.shape
    span = energies // 4 if energies % 4 == 0 else energies

    def lanes(part):
        return pl.ds(part, rows, stride=2)

    pltpu.make_async_copy(g, out_g.at[:, 0], sems.at[0]).start()
    for j in range(slabs):
        for e in range(energies):
            real = jnp.zeros((rows, size), F32)
            imag = jnp.zeros((rows, size), F32)
            for w in range(e + 1):
                gr, gi = landed[j, e - w, 0], landed[j, e - w, 1]
                sr, si = scr[j, w, lanes(0)], scr[j, w, lanes(1)]
                real = real + (gr * sr - gi * si)
                imag = imag + (gr * si + gi * sr)
            se[j, e, lanes(0)] = real
            se[j, e, lanes(1)] = imag
            if (e + 1) % span == 0:
                part = pl.ds(e + 1 - span, span)
                pltpu.make_async_copy(se.at[j, part], out_se.at[j, part], sems.at[1]).start()
    pltpu.make_async_copy(g, out_g.at[:, 0], sems.at[0]).wait()
    pltpu.make_async_copy(se, out_se, sems.at[1]).wait()


def body(retain, hopping, source, screened):
    slabs, _, _, size, _ = hopping.shape
    energies = screened.shape[1]
    rows = screened.shape[3] // size
    woven = (
        screened.reshape(slabs, energies, 2, rows, size)
        .transpose(0, 1, 3, 2, 4)
        .reshape(slabs, energies, 2 * rows, size)
    )
    any_spec = pl.BlockSpec(memory_space=pl.ANY)
    vmem_spec = pl.BlockSpec(memory_space=pltpu.VMEM)
    vmem = pltpu.VMEM
    greens, landed, kept = pl.pallas_call(
        kernel,
        out_shape=(
            vmem((slabs, 2, size, size), F32),
            vmem((slabs, energies, 2, rows, size), F32),
            vmem(woven.shape, F32),
        ),
        in_specs=[pl.BlockSpec(memory_space=pltpu.HBM)] * 4,
        out_specs=(vmem_spec,) * 3,
        scratch_shapes=[
            pltpu.SMEM((slabs,), F32),
            vmem((2, slabs, 2, size, size), F32),
            vmem((2 * slabs, OUTS, 4 * size // OUTS, 2 * size), BF16),
            vmem((2 * slabs, 2, 2 * size, 2 * size), BF16),
            vmem((slabs, 2 * size, size), F32),
            vmem((2, size, size), F32),
            vmem((2 * slabs, 2 * size, size), F32),
            vmem((2 * slabs, 2 * size, size), F32),
            vmem((2, 2 * size, size), F32),
            vmem((2, size, size), F32),
            vmem((slabs, 2, size, size), F32),
            vmem((2 * slabs, size, 2 * size), F32),
            pltpu.SemaphoreType.DMA((1,)),
            pltpu.SemaphoreType.DMA((2,)),
            pltpu.SemaphoreType.DMA((GROUPS,)),
            pltpu.SemaphoreType.DMA((GROUPS,)),
            pltpu.SemaphoreType.DMA((1,)),
            pltpu.SemaphoreType.DMA((slabs,)),
            pltpu.SemaphoreType.DMA((3,)),
            pltpu.SemaphoreType.REGULAR,
            pltpu.SemaphoreType.REGULAR((max(energies.bit_length() - 2, 1),)),
        ],
        compiler_params=pltpu.CompilerParams(
            collective_id=0, has_side_effects=True
        ),
    )(retain.reshape(slabs), hopping, source, woven)
    greens, self_energy = pl.pallas_call(
        write_out,
        out_shape=(
            jax.ShapeDtypeStruct(source.shape, F32),
            jax.ShapeDtypeStruct(woven.shape, F32),
        ),
        in_specs=[vmem_spec] * 3,
        out_specs=(any_spec, any_spec),
        scratch_shapes=[vmem(woven.shape, F32), pltpu.SemaphoreType.DMA((2,))],
        compiler_params=pltpu.CompilerParams(vmem_limit_bytes=4 << 20),
    )(greens, landed, kept)
    return greens, (
        self_energy.reshape(slabs, energies, rows, 2, size)
        .transpose(0, 1, 3, 2, 4)
        .reshape(screened.shape)
    )


def solution(mesh):
    placed = (
        P("space", "energy"),
        P("space", "energy", None, None, None),
        P("space", "energy", None, None, None),
        P("space", None, None, "energy"),
    )
    return jax.shard_map(
        body,
        mesh=mesh,
        in_specs=placed,
        out_specs=(P("space", "energy", None, None, None), P("space", None, None, "energy")),
        check_vma=False,
    )
```

```python
import functools

import jax
import jax.numpy as jnp
from jax import lax
from jax.experimental import pallas as pl
from jax.experimental.pallas import tpu as pltpu
from jax.sharding import PartitionSpec as P

MESH = pl.DeviceIdType.MESH
F32 = jnp.float32
BF16 = jnp.bfloat16
CHUNKS = 8
GROUPS = 4
OUTS = 4
ORDER = {6: 0, 7: 1, 4: 2, 5: 3, 2: 4, 3: 5, 1: 1 << 30}
LS = 4


def split(value):
    high = value.astype(BF16)
    return high, (value - high.astype(F32)).astype(BF16)


dot = functools.partial(
    lax.dot_general, dimension_numbers=(((1,), (0,)), ((), ())), preferred_element_type=F32
)


def rows_by(block, right):
    (high, low), (rh, rl) = split(block), right
    count = high.shape[0]
    both = dot(jnp.concatenate([high, low], 0), rh)
    return both[:count] + (dot(high, rl) + both[count:])


def left_form(real, imag):
    return jnp.concatenate(
        [jnp.concatenate([real, -imag], 1), jnp.concatenate([imag, real], 1)], 0
    )


def dagger_form(real, imag):
    real, imag = real.T, imag.T
    return jnp.concatenate(
        [jnp.concatenate([real, -imag], 1), jnp.concatenate([imag, real], 1)], 0
    )


def arranged(form):
    size = form.shape[0] // 2
    height = size // OUTS
    high, low = split(form)
    return [
        jnp.concatenate(
            [x[p * size + o * height : p * size + (o + 1) * height] for x in (high, low) for p in range(2)], 0
        )
        for o in range(OUTS)
    ]


def part_by(left, right):
    height, size = left.shape[0] // 4, right.shape[1] // 2
    product = dot(left[: 2 * height], right)
    other = dot(left[2 * height :], right[:, :size])
    both = product[:, :size] + (product[:, size:] + other)
    return both[:height], both[height:]


def parts_of(product):
    height, size = product.shape[0] // 4, product.shape[1] // 2
    cross = product[: 2 * height, size:] + product[2 * height :, :size]
    both = product[: 2 * height, :size] + cross
    return both[:height], both[height:]


def columns_by(left, block):
    right = stacked(block)
    parts = [part_by(x, right) for x in left]
    return jnp.concatenate([p[0] for p in parts] + [p[1] for p in parts], 0)


def stacked(block):
    return jnp.concatenate(split(block), 1)


def turned_block(turned):
    size = turned.shape[1] // 2
    return jnp.concatenate([turned[:, :size], turned[:, size:]], 0)


def kernel(
    retain_hbm, hop_hbm, src_hbm, scr_hbm, g, landed, scr,
    retain, slabs_in, lefts, rights, bases, entering, own, brought, early, guest, passed, spun,
    load_sem, chain_send, chain_recv, guest_recv, swap_send, swap_recv, ahead_sem, turn, ready,
):
    _, slabs, _, size, _ = slabs_in.shape
    energies, rows = landed.shape[1], landed.shape[3]
    space, energy = lax.axis_index("space"), lax.axis_index("energy")
    stages = lax.axis_size("space")
    piece, height, group = size // CHUNKS, size // OUTS, size // GROUPS
    last = slabs - 1
    paired = energies % 2 == 0
    power = energies & (energies - 1) == 0 and paired
    per = energies // OUTS
    quartered = power and per >= 2
    order = sorted(range(1, energies), key=lambda k: ORDER.get(k, k))
    hop, src = slabs_in.at[0], slabs_in.at[1]

    odd = lax.rem(space, 2) == 1
    middle = (space > 0) & (space < stages - 1)
    paired = paired and power
    if paired:
        partner = energy + 1 - 2 * lax.rem(energy, 2)
        second = lax.rem(energy, 2) == 0
    else:
        partner = energy
        second = energy < 0
    first = jnp.logical_not(second)
    hosts = first & (space > 0) & paired
    hosted = second & (space > 0)
    gives = second & middle & jnp.logical_not(odd)
    takes = hosts & odd & (space > 1)
    links = hosts & odd & middle
    leaps = links & (space + 2 < stages)

    loads = [
        pltpu.make_async_copy(retain_hbm, retain, swap_send.at[0]),
        *(
            pltpu.make_async_copy(
                array.at[which, 0, part, pl.ds(i * size // LS, size // LS)],
                ref.at[which, part, pl.ds(i * size // LS, size // LS)],
                chain_send.at[0],
            )
            for array, ref, which in (
                (hop_hbm, hop, slice(1, None)),
                (src_hbm, src, slice(0, 1)),
            )
            for part in range(2)
            for i in range(LS)
        ),
        pltpu.make_async_copy(src_hbm.at[1:, 0], src.at[1:], chain_send.at[1]),
        pltpu.make_async_copy(hop_hbm.at[:1, 0], hop.at[:1], chain_send.at[1]),
        pltpu.make_async_copy(scr_hbm, scr, load_sem.at[0]),
    ]
    for load in loads:
        load.start()

    barrier = pltpu.get_barrier_semaphore()

    def greet(where, who):
        pl.semaphore_signal(barrier, inc=1, device_id=(where, who), device_id_type=MESH)

    bits = [1 << b for b in range(energies.bit_length() - 1)] if power else []
    rounds = len(bits) - 1
    if power:
        for bit in bits:
            greet(space, jnp.bitwise_xor(energy, bit))
    else:
        for step in range(1, energies):
            greet(space, lax.rem(energy + step, energies))

    def call(level):
        if 0 < level <= rounds:
            for bit in bits:
                pl.semaphore_signal(
                    ready.at[level - 1],
                    inc=1,
                    device_id=(space, jnp.bitwise_xor(energy, bit)),
                    device_id_type=MESH,
                )

    def hear(level):
        if 0 < level <= rounds:
            pl.semaphore_wait(ready.at[level - 1], len(bits))
            call(level + 1)

    def hear_all():
        for level in range(1, rounds + 1):
            hear(level)

    @pl.when(first & (space > 0))
    def _():
        greet(space - 1, energy)

    if paired:
        @pl.when((hosts & (space == 1)) | takes)
        def _():
            greet(space - 1, partner)

        @pl.when(takes)
        def _():
            greet(space - 2, energy)

    greeted = (
        (len(bits) if power else energies - 1)
        + (first & (space < stages - 1)).astype(jnp.int32)
        + leaps.astype(jnp.int32)
        + (second & (space < stages - 1) & jnp.logical_not(odd)).astype(jnp.int32)
    )

    def enter():
        pl.semaphore_wait(barrier, greeted)
        call(1)

    loads[0].wait()
    pltpu.make_async_copy(hop, hop, chain_send.at[0]).wait()

    def settle():
        pltpu.make_async_copy(hop, hop, chain_send.at[1]).wait()

    eye = (
        lax.broadcasted_iota(jnp.int32, (size, size), 0)
        == lax.broadcasted_iota(jnp.int32, (size, size), 1)
    ).astype(F32)

    def coupler(j):
        factor = retain[j]
        return factor * (eye + hop[j, 0]), factor * hop[j, 1]

    def sandwich(left, right, block):
        wide = jnp.concatenate([block[:size], block[size:]], 1)
        return columns_by(left, turned_block(rows_by(wide, right)))

    def source(j):
        return jnp.concatenate([src[j, 0], src[j, 1]], 0)

    step_lefts, step_rights = [None], [None]
    for j in range(1, slabs):
        step_lefts.append(arranged(left_form(*coupler(j))))
        step_rights.append(split(dagger_form(*coupler(j))))

    def copy(source_ref, target_ref, sems, where, who):
        return pltpu.make_async_remote_copy(
            src_ref=source_ref,
            dst_ref=target_ref,
            send_sem=sems[0],
            recv_sem=sems[1],
            device_id=(where, who),
            device_id_type=MESH,
        )

    def line(source_ref, target_ref, recv, start, count, where, who, sem=0):
        lines = pl.ds(start, count)
        return copy(
            source_ref.at[:, lines],
            target_ref.at[:, lines],
            (chain_send.at[sem], recv.at[start // group]),
            where,
            who,
        )

    made = g.at[last]

    def send_on(begin, count, to_guest=False):
        for c in range(begin, begin + count):
            if to_guest:
                line(made, guest, guest_recv, c * piece, piece, space + 1, partner).start()
            else:
                line(made, entering, chain_recv, c * piece, piece, space + 1, energy, sem=int(c == 0)).start()

    def sent(count, sem=0):
        line(made, entering, chain_recv, 0, count, space, energy, sem=sem).wait_send()

    def ahead(i, where, who):
        return copy(
            own.at[i * slabs + last], early.at[i], (ahead_sem.at[0], ahead_sem.at[1]), where, who
        )

    def aheads():
        return copy(early, early, (ahead_sem.at[0], ahead_sem.at[1]), space, energy)

    def bring():
        return copy(own, brought, (ahead_sem.at[0], ahead_sem.at[2]), space, partner)

    def swap(j, peer, source=None, who=None):
        rows_of = pl.ds(pl.multiple_of(peer * rows, rows), rows)
        return copy(
            (g if source is None else source).at[j, :, rows_of],
            landed.at[j, energy if who is None else who],
            (swap_send.at[0], swap_recv.at[0]),
            space,
            peer,
        )

    def spread_guest(*js):
        for k in order:
            if k > 1:
                peer = jnp.bitwise_xor(energy - lax.rem(energy, 2), k)
                for j in js:
                    swap(j, peer, passed, partner).start()

    def spread(*js):
        for k in order:
            if not power:
                peer = lax.rem(energy + k, energies)
            elif k == 1:
                peer = jnp.bitwise_xor(energy, 1)
            else:
                peer = jnp.bitwise_xor(energy - lax.rem(energy, 2), k)
            for j in js:
                swap(j, peer).start()

    def keep(j, block):
        real, imag = block[:size], block[size:]
        for o, part in enumerate(arranged(left_form(real, imag))):
            lefts[j, o] = part
        rights[j, 0], rights[j, 1] = split(dagger_form(real, imag))

    def left_of(j):
        return [lefts[j, o] for o in range(OUTS)]

    def right_of(j):
        return rights[j, 0], rights[j, 1]

    def finish(target, o, left, inner, more):
        for part, value in enumerate(part_by(left, inner)):
            target[part, o * height : (o + 1) * height] = value + more(part)

    def base_part(j, o):
        return lambda part: bases[j, part * size + o * height : part * size + (o + 1) * height]

    def finish_all(j, inner, target=None, more=None):
        whole = jnp.concatenate(left_of(j), 0)
        product = dot(whole, inner)
        step = 4 * height
        for o in range(OUTS):
            for part, value in enumerate(parts_of(product[o * step : (o + 1) * step])):
                start = part * size + o * height
                if target is None:
                    g[j, part, o * height : (o + 1) * height] = value + base_part(j, o)(part)
                else:
                    target[part, o * height : (o + 1) * height] = (
                        value + more[start : start + height]
                    )

    def quarters(begin, inners, target, more, source_ref, who):
        for d in range(OUTS - 1, -1, -1):
            o = jnp.bitwise_xor(energy // per, d)
            at = pl.multiple_of(o * height, height)
            for j in range(last, -1, -1):
                for part, value in enumerate(part_by(lefts[begin + j, o], inners[j])):
                    target[j, part, pl.ds(at, height)] = (
                        value + more[begin + j, pl.ds(part * size + at, height)]
                    )
            if d:
                peers = [o * per + i for i in range(per)]
            else:
                peers = [jnp.bitwise_xor(energy, i) for i in range(2 if begin else 1, per)]
            for peer in peers:
                for j in range(last, -1, -1):
                    swap(j, peer, source_ref, who).start()

    def give_turn():
        pl.semaphore_signal(turn, inc=1, device_id=(space, partner), device_id_type=MESH)

    @pl.when(space == 0)
    def _():
        if last > 1:
            settle()
        base = source(0)
        for j in range(1, slabs):
            g[j - 1, 0] = base[:size]
            g[j - 1, 1] = base[size:]
            if j < last:
                base = sandwich(step_lefts[j], step_rights[j], base) + source(j)
        wide = jnp.concatenate([base[:size], base[size:]], 1)
        inner = stacked(turned_block(rows_by(wide, step_rights[last])))
        if last < 2:
            settle()
        for o in range(OUTS):
            lines = slice(o * height, (o + 1) * height)
            finish(
                made,
                o,
                step_lefts[last][o],
                inner,
                lambda part: src[last, part, lines],
            )
            if o == 0:
                enter()
            if stages > 1:
                @pl.when(first)
                def _():
                    send_on(o * CHUNKS // OUTS, CHUNKS // OUTS)
        if stages > 1 and paired:
            @pl.when(second)
            def _():
                pl.semaphore_wait(turn, 1)
                send_on(0, CHUNKS, True)
                give_turn()

            @pl.when(first)
            def _():
                sent(piece, 1)
                give_turn()
                pl.semaphore_wait(turn, 1)

        hear_all()
        spread(*range(last, -1, -1))

    @pl.when(space > 0)
    def _():
        settle()
        block = jnp.concatenate(coupler(0), 0)
        for j in range(slabs):
            if j > 0:
                block = columns_by(step_lefts[j], block)
            keep(j, block)
            own[j] = block
        enter()

        if paired:
            @pl.when(gives)
            def _():
                ahead(0, space + 1, partner).start()

        base = source(0)
        bases[0] = base
        own[slabs] = base
        for j in range(1, slabs):
            base = sandwich(step_lefts[j], step_rights[j], base) + source(j)
            bases[j] = base
            own[slabs + j] = base
        if paired:
            @pl.when(gives)
            def _():
                ahead(1, space + 1, partner).start()

            @pl.when(hosted)
            def _():
                bring().start()

        @pl.when(hosted | jnp.logical_not(odd & middle))
        def _():
            hear_all()

        def gather(source_ref, recv, begin):
            for c in range(GROUPS):
                line(made, source_ref, recv, c * group, group, space, energy).wait_recv()
                if c < GROUPS - 1:
                    lines = pl.ds(c * group, group)
                    arrived = jnp.concatenate([source_ref[0, lines], source_ref[1, lines]], 1)
                    for j in range(last, -1, -1):
                        spun[begin + j, lines] = rows_by(arrived, right_of(begin + j))

        def inner_of(source_ref, begin, j):
            lines = pl.ds(size - group, group)
            arrived = jnp.concatenate([source_ref[0, lines], source_ref[1, lines]], 1)
            tail = rows_by(arrived, right_of(begin + j))
            return stacked(turned_block(jnp.concatenate([spun[begin + j, : size - group], tail], 0)))

        def own_part():
            gather(entering, chain_recv, 0)

            @pl.when(space == stages - 1)
            def _():
                inners = [inner_of(entering, 0, j) for j in range(slabs)]
                if quartered:
                    quarters(0, inners, g, bases, None, None)
                else:
                    for j in range(last, -1, -1):
                        finish_all(j, inners[j])
                    spread(*range(last, -1, -1))

            @pl.when(middle)
            def _():
                inner = inner_of(entering, 0, last)
                for o in range(OUTS):
                    finish(made, o, lefts[last, o], inner, base_part(last, o))
                    send_on(o * CHUNKS // OUTS, CHUNKS // OUTS)

        def own_rest():
            @pl.when(middle)
            def _():
                for j in range(last - 1, -1, -1):
                    finish_all(j, inner_of(entering, 0, j))

        def welcome():
            bring().wait_recv()
            for j in range(slabs):
                keep(slabs + j, brought[j])

        def guest_part():
            gather(guest, guest_recv, slabs)

            @pl.when(jnp.logical_not(odd & middle))
            def _():
                inners = [inner_of(guest, slabs, j) for j in range(slabs)]
                if quartered:
                    quarters(slabs, inners, passed, brought, passed, partner)
                else:
                    for j in range(last, -1, -1):
                        finish_all(slabs + j, inners[j], passed.at[j], brought.at[slabs + j])
                    spread_guest(*range(last, -1, -1))
                copy(passed, g, (chain_send.at[0], chain_recv.at[0]), space, partner).start()

            @pl.when(odd & middle)
            def _():
                inner = inner_of(guest, slabs, last)
                out = passed.at[last]
                for o in range(OUTS):
                    finish(
                        out,
                        o,
                        lefts[slabs + last, o],
                        inner,
                        lambda part: brought[
                            slabs + last,
                            part * size + o * height : part * size + (o + 1) * height,
                        ],
                    )

                    @pl.when(leaps)
                    def _():
                        for c in range(o * CHUNKS // OUTS, (o + 1) * CHUNKS // OUTS):
                            line(out, guest, guest_recv, c * piece, piece, space + 2, energy).start()

                for c in range(CHUNKS):
                    line(out, guest, guest_recv, c * piece, piece, space + 1, energy).start()
                for j in range(last - 1, -1, -1):
                    finish_all(
                        slabs + j, inner_of(guest, slabs, j), passed.at[j], brought.at[slabs + j]
                    )
                copy(passed, g, (chain_send.at[0], chain_recv.at[0]), space, partner).start()

        if not paired:
            own_part()
            own_rest()
            @pl.when(middle)
            def _():
                spread(*range(last, -1, -1))
        else:
            @pl.when(takes)
            def _():
                welcome()
                aheads().wait_recv()
                for j in range(slabs):
                    left = left_of(slabs + j)
                    brought[slabs + j] = (
                        sandwich(left, right_of(slabs + j), early[1]) + brought[slabs + j]
                    )
                    keep(slabs + j, columns_by(left, early[0]))
                guest_part()

            @pl.when(first)
            def _():
                own_part()

            @pl.when(first & middle & jnp.logical_not(odd))
            def _():
                own_rest()
                spread(*range(last, -1, -1))

            @pl.when(hosts & jnp.logical_not(takes))
            def _():
                welcome()
                guest_part()

            @pl.when(links)
            def _():
                hear_all()
                spread(last)
                own_rest()
                spread(*range(last - 1, -1, -1))
                spread_guest(*range(last, -1, -1))

            @pl.when(hosts)
            def _():
                for j in range(slabs):
                    landed[j, partner] = passed[j, :, pl.ds(pl.multiple_of(energy * rows, rows), rows)]

            @pl.when(hosted)
            def _():
                copy(passed, g, (chain_send.at[0], chain_recv.at[0]), space, energy).wait_recv()

    loads[-1].wait()
    mine = pl.ds(pl.multiple_of(energy * rows, rows), rows)
    for j in range(slabs):
        landed[j, energy] = g[j, :, mine]
    for count, there in ((energies - 2, hosts), (energies - 1, jnp.logical_not(hosts))):
        @pl.when(there)
        def _():
            others = landed.at[:, pl.ds(0, count)]
            pltpu.make_async_copy(others, others, swap_recv.at[0]).wait()

    others = landed.at[:, pl.ds(0, energies - 1)]
    fewer = landed.at[:, pl.ds(0, energies - 2)]

    @pl.when(jnp.logical_not(hosted))
    def _():
        pltpu.make_async_copy(others, others, swap_send.at[0]).wait()

    @pl.when(first & (space < stages - 1))
    def _():
        sent(size - piece)
        if not paired:
            sent(piece, 1)

    if paired:
        @pl.when(first & middle)
        def _():
            sent(piece, 1)

        @pl.when(hosted)
        def _():
            bring().wait_send()

        @pl.when(gives)
        def _():
            aheads().wait_send()

        @pl.when(second & (space == 0) & (stages > 1))
        def _():
            sent(size)

        @pl.when(hosts)
        def _():
            pltpu.make_async_copy(fewer, fewer, swap_send.at[0]).wait()
            copy(passed, g, (chain_send.at[0], chain_recv.at[0]), space, partner).wait_send()

        @pl.when(links)
        def _():
            sent(size)

        @pl.when(leaps)
        def _():
            sent(size)


def write_out(g, landed, scr, out_g, out_se, se, sems):
    slabs, energies, _, rows, size = landed.shape
    span = energies // 4 if energies % 4 == 0 else energies

    def lanes(part):
        return pl.ds(part, rows, stride=2)

    pltpu.make_async_copy(g, out_g.at[:, 0], sems.at[0]).start()
    for j in range(slabs):
        for e in range(energies):
            real = jnp.zeros((rows, size), F32)
            imag = jnp.zeros((rows, size), F32)
            for w in range(e + 1):
                gr, gi = landed[j, e - w, 0], landed[j, e - w, 1]
                sr, si = scr[j, w, lanes(0)], scr[j, w, lanes(1)]
                real = real + (gr * sr - gi * si)
                imag = imag + (gr * si + gi * sr)
            se[j, e, lanes(0)] = real
            se[j, e, lanes(1)] = imag
            if (e + 1) % span == 0:
                part = pl.ds(e + 1 - span, span)
                pltpu.make_async_copy(se.at[j, part], out_se.at[j, part], sems.at[1]).start()
    pltpu.make_async_copy(g, out_g.at[:, 0], sems.at[0]).wait()
    pltpu.make_async_copy(se, out_se, sems.at[1]).wait()


def body(retain, hopping, source, screened):
    slabs, _, _, size, _ = hopping.shape
    energies = screened.shape[1]
    rows = screened.shape[3] // size
    woven = (
        screened.reshape(slabs, energies, 2, rows, size)
        .transpose(0, 1, 3, 2, 4)
        .reshape(slabs, energies, 2 * rows, size)
    )
    any_spec = pl.BlockSpec(memory_space=pl.ANY)
    vmem_spec = pl.BlockSpec(memory_space=pltpu.VMEM)
    vmem = pltpu.VMEM
    greens, landed, kept = pl.pallas_call(
        kernel,
        out_shape=(
            vmem((slabs, 2, size, size), F32),
            vmem((slabs, energies, 2, rows, size), F32),
            vmem(woven.shape, F32),
        ),
        in_specs=[pl.BlockSpec(memory_space=pltpu.HBM)] * 4,
        out_specs=(vmem_spec,) * 3,
        scratch_shapes=[
            pltpu.SMEM((slabs,), F32),
            vmem((2, slabs, 2, size, size), F32),
            vmem((2 * slabs, OUTS, 4 * size // OUTS, 2 * size), BF16),
            vmem((2 * slabs, 2, 2 * size, 2 * size), BF16),
            vmem((slabs, 2 * size, size), F32),
            vmem((2, size, size), F32),
            vmem((2 * slabs, 2 * size, size), F32),
            vmem((2 * slabs, 2 * size, size), F32),
            vmem((2, 2 * size, size), F32),
            vmem((2, size, size), F32),
            vmem((slabs, 2, size, size), F32),
            vmem((2 * slabs, size, 2 * size), F32),
            pltpu.SemaphoreType.DMA((1,)),
            pltpu.SemaphoreType.DMA((2,)),
            pltpu.SemaphoreType.DMA((GROUPS,)),
            pltpu.SemaphoreType.DMA((GROUPS,)),
            pltpu.SemaphoreType.DMA((1,)),
            pltpu.SemaphoreType.DMA((1,)),
            pltpu.SemaphoreType.DMA((3,)),
            pltpu.SemaphoreType.REGULAR,
            pltpu.SemaphoreType.REGULAR((max(energies.bit_length() - 2, 1),)),
        ],
        compiler_params=pltpu.CompilerParams(
            collective_id=0, has_side_effects=True
        ),
    )(retain.reshape(slabs), hopping, source, woven)
    greens, self_energy = pl.pallas_call(
        write_out,
        out_shape=(
            jax.ShapeDtypeStruct(source.shape, F32),
            jax.ShapeDtypeStruct(woven.shape, F32),
        ),
        in_specs=[vmem_spec] * 3,
        out_specs=(any_spec, any_spec),
        scratch_shapes=[vmem(woven.shape, F32), pltpu.SemaphoreType.DMA((2,))],
        compiler_params=pltpu.CompilerParams(vmem_limit_bytes=4 << 20),
    )(greens, landed, kept)
    return greens, (
        self_energy.reshape(slabs, energies, rows, 2, size)
        .transpose(0, 1, 3, 2, 4)
        .reshape(screened.shape)
    )


def solution(mesh):
    placed = (
        P("space", "energy"),
        P("space", "energy", None, None, None),
        P("space", "energy", None, None, None),
        P("space", None, None, "energy"),
    )
    return jax.shard_map(
        body,
        mesh=mesh,
        in_specs=placed,
        out_specs=(P("space", "energy", None, None, None), P("space", None, None, "energy")),
        check_vma=False,
    )
```
